128 devices in a mesh: gx: 8 (over y_lo, z), gy: 16 (over y_hi, x, core).
Axes of the slice: x: 4, y: 4 (y_hi: 2, y_lo: 2; y = y_hi * 2 + y_lo), z: 4, core: 2. Of those that a mesh axis runs over, the one named last changes fastest.
Arguments:
- thickness: float32 [4096, 2048], P('gy', 'gx'), may hold values from 0.5 to 2
- driving: float32 [2, 4096, 2048], P(None, 'gy', 'gx'), may hold values from -6 to 6
- observed: float32 [2, 4096, 2048], P(None, 'gy', 'gx'), may hold values from -2 to 2
- control: float32 [64, 4096], P('gy'), may hold values from 0.5 to 1.5
- ice_mask: int32 [16, 8], replicated, may hold values 0 or 1
- tile_block: int32 [16, 8, 1], replicated, may hold values from 0 to 63
Outputs:
- vel_u: float32 [4096, 2048], P('gy', 'gx')
- vel_v: float32 [4096, 2048], P('gy', 'gx')
- grad_control: float32 [64, 4096], P('gy')
The draws below stay inside these ranges and needn't reach their ends.
Inputs may be any that keep to these rules, and one draw needn't show every extreme that they name: `tile_block`: every one of the 64 control blocks is named by at least one tile.
All inputs are finite; a program needn't handle non-finite values.
Results may differ from the reference program's by a relative error of at most 0.00015.
Values sent between devices are 32-bit elements; how exact they have to be, the bound alone decides.
A program may use at most 64 MiB of HBM per device.

```python
import math
import jax
import jax.numpy as jnp
from jax import lax

TILE = 256
CPC = 4
PIC = 4
SW = 2
ADJ = 6
CT = 64
COARSE = 4096
TY = 16
TX = 8
NY = 4096
NX = 2048
K = 64


def place_ends(array, rng, least, top_value):
    index_at = [jax.random.randint(jax.random.fold_in(rng, axis), (), 0, length) for axis, length in enumerate(array.shape)]
    main_axis = array.shape.index(max(array.shape))
    neighbour = index_at[:main_axis] + [(index_at[main_axis] + 1) % array.shape[main_axis]] + index_at[main_axis + 1:]
    return array.at[tuple(index_at)].set(least).at[tuple(neighbour)].set(top_value)


def levels(rng, extent, cuts, least, largest):
    factor_of = 1.0
    for dim, blocks in cuts:
        heights = jax.random.uniform(jax.random.fold_in(jax.random.fold_in(rng, 6), dim), (blocks,), jnp.float32, least / len(cuts), largest / len(cuts))
        factor_of = factor_of * jnp.repeat(jnp.exp(heights), extent[dim] // blocks).reshape((-1,) + (1,) * (len(extent) - 1 - dim))
    return factor_of


def choose_distinct(rng, rows, count, top, lift):
    order = jax.random.permutation(jax.random.fold_in(rng, 1), count)
    favour = order
    for power in range(3):
        favour = favour * favour // count
    favour = favour * lift // count
    lots = jax.random.randint(jax.random.fold_in(rng, 2), (rows, count), 0, 4096) + favour
    sure = jax.random.permutation(jax.random.fold_in(rng, 3), rows)[jnp.arange(count) % rows]
    lots = jnp.where(jnp.arange(rows)[:, None] == sure[None, :], 1 << 14, lots)
    score = lots * count + jnp.arange(count)
    return lax.top_k(score.astype(jnp.int32), top)[1].astype(jnp.int32)


def gaussian(stream_key, shape, width, limit, cuts=(), dtype=jnp.bfloat16):
    values = jax.random.normal(stream_key, shape, jnp.float32) * width
    if len(cuts) > 0:
        values = levels(stream_key, shape, cuts, -0.22, 0.18) * values
    return jnp.clip(values, min=-limit, max=limit).astype(dtype)


def setup_inputs(seed: int = 0) -> dict:
    streams_of = jax.random.split(jax.random.key(seed), 7)
    thickness = jnp.clip(jnp.exp(math.log(2.0) - 1.3862944 * jax.random.uniform(streams_of[0], (NY, NX), jnp.float32) ** levels(streams_of[0], (NY, NX), ((0, 16), (1, 8)), -0.2, 0.2)), 0.5, 2.0)
    driving = gaussian(streams_of[1], (2, NY, NX), 1.0, 6.0, ((1, 16), (2, 8)), jnp.float32)
    observed = gaussian(streams_of[2], (2, NY, NX), 0.3, 2.0, ((1, 16), (2, 8)), jnp.float32)
    control = jnp.clip(0.5 + 1.0 * jax.random.uniform(streams_of[3], (K, COARSE), jnp.float32) ** levels(streams_of[3], (K, COARSE), ((0, 16),), -0.2, 0.2), 0.5, 1.5)
    ice_mask = place_ends((jax.random.randint(streams_of[4], (TY, TX), 0, 4) < 3).astype(jnp.int32), jax.random.fold_in(streams_of[4], 1), 0, 1)
    tile_block = choose_distinct(streams_of[5], TY * TX, K, 1, 256).reshape((TY, TX, 1))
    return dict(thickness=thickness, driving=driving, observed=observed, control=control, ice_mask=ice_mask, tile_block=tile_block)


visc_scale = 0.1
strain_floor = 0.05


def viscosity(vel_pad, thick):
    speed_x = vel_pad[0]
    speed_y = vel_pad[1]
    dudx = 0.5 * (speed_x[1:-1, 2:] - speed_x[1:-1, :-2])
    dudy = 0.5 * (speed_x[2:, 1:-1] - speed_x[:-2, 1:-1])
    dvdx = 0.5 * (speed_y[1:-1, 2:] - speed_y[1:-1, :-2])
    dvdy = 0.5 * (speed_y[2:, 1:-1] - speed_y[:-2, 1:-1])
    shear = dudy + dvdx
    strain = dudx * dudx + dvdy * dvdy + dudx * dvdy + 0.25 * shear * shear + strain_floor
    return visc_scale * thick * jnp.power(strain, -1.0 / 3.0)


def coefficients(visc_pad, friction):
    center = visc_pad[1:-1, 1:-1]
    east_w = 0.5 * (center + visc_pad[1:-1, 2:])
    west_w = 0.5 * (center + visc_pad[1:-1, :-2])
    south_w = 0.5 * (center + visc_pad[2:, 1:-1])
    north_w = 0.5 * (center + visc_pad[:-2, 1:-1])
    diag_u = friction + 4.0 * (east_w + west_w) + south_w + north_w
    diag_v = friction + east_w + west_w + 4.0 * (south_w + north_w)
    return (visc_pad, east_w, west_w, south_w, north_w, diag_u, diag_v)


def relaxation(vel_pad, stencil_coef, forcing, ice_cells):
    visc_pad, east_w, west_w, south_w, north_w, diag_u, diag_v = stencil_coef
    speed_x = vel_pad[0]
    speed_y = vel_pad[1]
    flux_p = 2.0 * visc_pad[1:-1, :] * (0.5 * (speed_y[2:, :] - speed_y[:-2, :]))
    flux_q = visc_pad[:, 1:-1] * (0.5 * (speed_y[:, 2:] - speed_y[:, :-2]))
    cross_u = 0.5 * (flux_p[:, 2:] - flux_p[:, :-2]) + 0.5 * (flux_q[2:, :] - flux_q[:-2, :])
    flux_r = 2.0 * visc_pad[:, 1:-1] * (0.5 * (speed_x[:, 2:] - speed_x[:, :-2]))
    flux_s = visc_pad[1:-1, :] * (0.5 * (speed_x[2:, :] - speed_x[:-2, :]))
    cross_v = 0.5 * (flux_r[2:, :] - flux_r[:-2, :]) + 0.5 * (flux_s[:, 2:] - flux_s[:, :-2])
    near_u = 4.0 * (east_w * speed_x[1:-1, 2:] + west_w * speed_x[1:-1, :-2]) + south_w * speed_x[2:, 1:-1] + north_w * speed_x[:-2, 1:-1]
    near_v = east_w * speed_y[1:-1, 2:] + west_w * speed_y[1:-1, :-2] + 4.0 * (south_w * speed_y[2:, 1:-1] + north_w * speed_y[:-2, 1:-1])
    new_u = ice_cells * (forcing[0] + near_u + cross_u) / diag_u
    new_v = ice_cells * (forcing[1] + near_v + cross_v) / diag_v
    return jnp.stack([new_u, new_v])


def pad_cells(field):
    return jnp.pad(field, ((0, 0), (1, 1), (1, 1)))


def reference(thickness, driving, observed, control, ice_mask, tile_block):
    blocks = tile_block[:, :, 0].astype(jnp.int32)
    rates = jnp.exp(control)[blocks]
    friction = jnp.broadcast_to(rates.reshape(TY, TX, CT, 1, CT, 1), (TY, TX, CT, CPC, CT, CPC))
    friction = friction.reshape(TY, TX, TILE, TILE).transpose(0, 2, 1, 3).reshape(NY, NX)
    ice_cells = jnp.broadcast_to(ice_mask.astype(jnp.float32)[:, None, :, None], (TY, TILE, TX, TILE)).reshape(NY, NX)
    velocity = jnp.zeros((2, NY, NX), jnp.float32)
    stencil_coef = None
    for picard in range(PIC):
        visc_cells = viscosity(pad_cells(velocity), thickness)
        stencil_coef = coefficients(jnp.pad(visc_cells, 1), friction)
        for sweep in range(SW):
            velocity = relaxation(pad_cells(velocity), stencil_coef, driving, ice_cells)
    misfit = ice_cells * (velocity - observed)
    adjoint = jnp.zeros((2, NY, NX), jnp.float32)
    for sweep in range(ADJ):
        adjoint = relaxation(pad_cells(adjoint), stencil_coef, misfit, ice_cells)
    cell_grad = -friction * (velocity[0] * adjoint[0] + velocity[1] * adjoint[1])
    tile_grad = cell_grad.reshape(TY, CT, CPC, TX, CT, CPC).sum(axis=(2, 5))
    tile_grad = tile_grad.transpose(0, 2, 1, 3).reshape(TY * TX, COARSE)
    gradient = jax.ops.segment_sum(tile_grad, blocks.reshape(-1), num_segments=K)
    return velocity[0], velocity[1], gradient
```

```python
import functools

import jax
import jax.numpy as jnp
import numpy as np
from jax import lax
from jax.experimental import pallas as pl
from jax.experimental.pallas import tpu as pltpu
from jax.sharding import PartitionSpec as P

TILE = 256
HALO = 16
EXT = TILE + 2 * HALO
STRIP = EXT // 8
LT = 3
PIC = 4
ADJ = 6
GX = 8
GY = 16
UNROLL = 3
MESH = pl.DeviceIdType.MESH
F32 = jnp.float32

visc_scale = 0.1
strain_floor = 0.05


def exchange_kernel(
    blk, thick, drv, obs, ctl,
    h_north, h_south, h_west, h_east, coarse,
    pack_w, pack_e, c_send, c_recv,
    g_send, g_recv, x_send, x_recv, n_send, n_recv,
):
    gx = lax.axis_index("gx")
    gy = lax.axis_index("gy")

    def dev(dy, dx):
        return (lax.rem(gx + dx + GX, GX), lax.rem(gy + dy + GY, GY))

    barrier = pltpu.get_barrier_semaphore()
    peers = [(dy, 0) for dy in range(1, GY)] + [(dy, dx) for dx in (-1, 1) for dy in (-1, 0, 1)]
    for dy, dx in peers:
        pl.semaphore_signal(barrier, inc=1, device_id=dev(dy, dx), device_id_type=MESH)

    for off in range(GY):
        dest = lax.rem(gy + off, GY)
        c_send[off] = ctl[lax.rem(blk[dest, gx], 4)]
    c_recv[0] = c_send[0]

    lane = lax.broadcasted_iota(jnp.int32, (8, 128), 1)

    @pl.loop(0, TILE // 8)
    def _(t):
        rows = pl.ds(pl.multiple_of(t * 8, 8), 8)
        fields = [thick, drv.at[0], drv.at[1], obs.at[0], obs.at[1]]
        west = fields[0][rows, pl.ds(0, 128)]
        east = fields[0][rows, pl.ds(128, 128)]
        for f in range(1, 5):
            west = jnp.where(lane < 16 * f, west, pltpu.roll(fields[f][rows, pl.ds(0, 128)], 16 * f, 1))
            east = jnp.where(
                lane >= 128 - 16 * f, east, pltpu.roll(fields[f][rows, pl.ds(128, 128)], 128 - 16 * f, 1)
            )
        pack_w[rows, :] = west
        pack_e[rows, :] = east

    pl.semaphore_wait(barrier, len(peers))

    def remote(src, dst, ss, rs, to):
        return pltpu.make_async_remote_copy(
            src_ref=src, dst_ref=dst, send_sem=ss, recv_sem=rs, device_id=to, device_id_type=MESH
        )

    gathers = [
        remote(c_send.at[off], c_recv.at[off], g_send.at[off], g_recv.at[off], dev(off, 0))
        for off in range(1, GY)
    ]
    for g in gathers:
        g.start()

    lo, hi, full = pl.ds(0, HALO), pl.ds(TILE - HALO, HALO), pl.ds(0, TILE)
    moves = [
        (pack_e, h_west.at[pl.ds(HALO, TILE)], (0, 1)),
        (pack_w, h_east.at[pl.ds(HALO, TILE)], (0, -1)),
        (thick.at[hi], h_north.at[0], (1, 0)),
        (thick.at[lo], h_south.at[0], (-1, 0)),
        (drv.at[:, hi], h_north.at[pl.ds(1, 2)], (1, 0)),
        (drv.at[:, lo], h_south.at[pl.ds(1, 2)], (-1, 0)),
        (obs.at[:, hi], h_north.at[pl.ds(3, 2)], (1, 0)),
        (obs.at[:, lo], h_south.at[pl.ds(3, 2)], (-1, 0)),
        (pack_e.at[hi], h_west.at[pl.ds(0, HALO)], (1, 1)),
        (pack_e.at[lo], h_west.at[pl.ds(TILE + HALO, HALO)], (-1, 1)),
        (pack_w.at[hi], h_east.at[pl.ds(0, HALO)], (1, -1)),
        (pack_w.at[lo], h_east.at[pl.ds(TILE + HALO, HALO)], (-1, -1)),
    ]
    halos = [
        remote(src, dst, x_send.at[n], x_recv.at[n], dev(*to)) for n, (src, dst, to) in enumerate(moves)
    ]
    for h in halos:
        h.start()

    for g in gathers:
        g.wait_recv()
    mine = blk[gy, gx]
    coarse[4] = c_recv[lax.rem(gy - mine // 4 + GY, GY)]
    near = []
    for dy in (-1, 0, 1):
        for dx in (-1, 0, 1):
            if (dy, dx) != (0, 0):
                slot = (1 - dy) * 3 + (1 - dx)
                near.append(
                    remote(coarse.at[4], coarse.at[slot], n_send.at[slot], n_recv.at[slot], dev(dy, dx))
                )
    for n in near:
        n.start()
    for h in halos:
        h.wait()
    for n in near:
        n.wait()
    for g in gathers:
        g.wait_send()


def solve_kernel(
    ice_ref, thick, drv, obs, h_north, h_south, h_west, h_east, coarse,
    out_u, out_v, grad,
    nat, cext, T, FU, FV, OU, OV, FR, IC, H, A, B, IU, IV,
    U0, UE0, UW0, V0, VE0, VW0, U1, UE1, UW1, V1, VE1, VW1,
):
    gx = lax.axis_index("gx")
    gy = lax.axis_index("gy")
    lane = lax.broadcasted_iota(jnp.int32, (8, 128), 1)
    sub = lax.broadcasted_iota(jnp.int32, (8, 128), 0)
    lane3 = lax.broadcasted_iota(jnp.int32, (LT, 8, 128), 2)
    sides = ((-1, -1), (-1, 0), (-1, 1), (0, -1), (0, 0), (0, 1), (1, -1), (1, 0), (1, 1))
    inside, iced = {}, {}
    for dy, dx in sides:
        ok = (gy + dy >= 0) & (gy + dy < GY) & (gx + dx >= 0) & (gx + dx < GX)
        flag = ok.astype(F32)
        at = ice_ref[jnp.clip(gy + dy, 0, GY - 1), jnp.clip(gx + dx, 0, GX - 1)]
        inside[dy, dx] = flag
        iced[dy, dx] = flag * at.astype(F32)

    def region(i, table):
        row = sub * STRIP + i

        def by_row(dx):
            return jnp.where(
                row < HALO, table[-1, dx], jnp.where(row < HALO + TILE, table[0, dx], table[1, dx])
            )

        center = by_row(0)
        edge = jnp.where(lane < HALO, by_row(1), jnp.where(lane >= 128 - HALO, by_row(-1), 0.0))
        return jnp.stack([center, center, edge])

    def west(x):
        y = pltpu.roll(x, 1, 2)
        return jnp.where(lane3 == 0, jnp.concatenate([y[2:], y[:2]], axis=0), y)

    def east(x):
        y = pltpu.roll(x, 127, 2)
        return jnp.where(lane3 == 127, jnp.concatenate([y[1:], y[:1]], axis=0), y)

    def wrap(refs):
        for ref in refs:
            ref[0] = pltpu.roll(ref[STRIP], 1, 1)
            ref[STRIP + 1] = pltpu.roll(ref[1], 7, 1)

    fields = [(thick, T), (drv.at[0], FU), (drv.at[1], FV), (obs.at[0], OU), (obs.at[1], OV)]
    for f, (src, dst) in enumerate(fields):
        for c in range(2):
            cols = pl.ds(c * 128, 128)
            nat[c, pl.ds(0, HALO)] = h_north[f, :, cols]
            nat[c, pl.ds(HALO, TILE)] = src[:, cols]
            nat[c, pl.ds(HALO + TILE, HALO)] = h_south[f, :, cols]

        @pl.loop(0, EXT // 8)
        def _(t):
            rows = pl.ds(pl.multiple_of(t * 8, 8), 8)
            right = h_east[rows, :]
            left = h_west[rows, :]
            if f > 0:
                right = pltpu.roll(right, 128 - 16 * f, 1)
                left = pltpu.roll(left, 16 * f, 1)
            nat[2, rows] = jnp.where(lane < HALO, right, jnp.where(lane >= 128 - HALO, left, 0.0))

        @pl.loop(0, STRIP)
        def _(i):
            x = jnp.stack([nat[c, pl.ds(i, 8, stride=STRIP), :] for c in range(LT)])
            if f == 0:
                x = x * region(i, inside)
                IC[i] = region(i, iced)
            dst[i] = x

    cext[...] = jnp.zeros_like(cext)
    for g, dx in enumerate((0, 1, -1)):
        cext[g, pl.ds(0, 2)] = jnp.exp(coarse[0 * 3 + 1 + dx, pl.ds(30, 2), :])
        cext[g, pl.ds(2, 32)] = jnp.exp(coarse[1 * 3 + 1 + dx])
        cext[g, pl.ds(34, 2)] = jnp.exp(coarse[2 * 3 + 1 + dx, pl.ds(0, 2), :])

    def hot(rows, cols, fn):
        r = lax.broadcasted_iota(jnp.int32, (rows, cols), 0)
        c = lax.broadcasted_iota(jnp.int32, (rows, cols), 1)
        return jnp.where(fn(r, c), 1.0, 0.0).astype(F32)

    def mul(a, b):
        return jnp.dot(a, b, precision=lax.Precision.HIGHEST, preferred_element_type=F32)

    wide = []
    for par in range(2):
        spread_c = hot(128, TILE, lambda r, c: r == par * 64 + c // 4)
        spread_e = hot(128, 128, lambda r, c: (c < HALO) & (r == par * 64 + c // 4))
        spread_w = hot(128, 128, lambda r, c: (c >= 128 - HALO) & (r == par * 64 + 60 + (c - 112) // 4))
        core = mul(cext[0], spread_c)
        edge = mul(cext[1], spread_e) + mul(cext[2], spread_w)
        wide.append(jnp.concatenate([core, edge], axis=1))
    wide = jnp.concatenate(wide, axis=0)
    tall = hot(EXT, 80, lambda r, c: ((r % 8) * STRIP + r // 8) // 4 == 2 * (c % 40) + c // 40)
    fine = mul(tall, wide)
    for c in range(LT):
        part = fine[:, c * 128:(c + 1) * 128].reshape(STRIP, 8, 128)
        if c == 2:
            part = jnp.where(part == 0.0, 1.0, part)
        FR[:, c] = part

    base = float(visc_scale * np.power(strain_floor, -1.0 / 3.0))

    def faces(first, src, last_rows):
        @pl.loop(0, STRIP)
        def _(i):
            if first:
                m = (0.5 * base) * T[i]
            else:
                U, UE, UW, V, VE, VW = src
                ux = 0.5 * (UE[i + 1] - UW[i + 1])
                vx = 0.5 * (VE[i + 1] - VW[i + 1])
                uy = 0.5 * (U[i + 2] - U[i])
                vy = 0.5 * (V[i + 2] - V[i])
                sh = uy + vx
                strain = ux * ux + vy * vy + ux * vy + 0.25 * (sh * sh) + strain_floor
                m = (0.5 * visc_scale) * T[i] * jnp.exp2(jnp.log2(strain) * (-1.0 / 3.0))
            H[i + 1] = m
            A[i] = east(m)
            B[i] = west(m)

        wrap([H])

        @pl.loop(0, STRIP)
        def _(i):
            h = H[i + 1]
            ew = 2.0 * h + A[i] + B[i]
            sn = 2.0 * h + H[i] + H[i + 2]
            fr = FR[i]
            ice = IC[i]
            iu = ice / (fr + 4.0 * ew + sn)
            iv = ice / (fr + ew + 4.0 * sn)
            IU[i] = iu
            IV[i] = iv
            if first:
                put(last_rows, i, iu * FU[i], iv * FV[i])

        if first:
            wrap(last_rows)

    def put(dst, i, u, v):
        U, UE, UW, V, VE, VW = dst
        U[i + 1] = u
        UE[i + 1] = east(u)
        UW[i + 1] = west(u)
        V[i + 1] = v
        VE[i + 1] = east(v)
        VW[i + 1] = west(v)

    def sweep(src, dst, fu_ref, fv_ref):
        U, UE, UW, V, VE, VW = src

        @pl.loop(0, STRIP // UNROLL)
        def _(it):
            b = it * UNROLL
            new_u = [[None] * LT for _ in range(UNROLL)]
            new_v = [[None] * LT for _ in range(UNROLL)]
            n = UNROLL + 2
            for c in range(LT):
                u = [U[b + j, c] for j in range(n)]
                ue = [UE[b + j, c] for j in range(n)]
                uw = [UW[b + j, c] for j in range(n)]
                v = [V[b + j, c] for j in range(n)]
                ve = [VE[b + j, c] for j in range(n)]
                vw = [VW[b + j, c] for j in range(n)]
                h = [H[b + j, c] for j in range(n)]
                q = [h[j] * (ve[j] - vw[j]) for j in range(n)]
                r = [h[j] * (ue[j] - uw[j]) for j in range(n)]
                face = [h[j] + h[j + 1] for j in range(n - 1)]
                for k in range(UNROLL):
                    j = k + 1
                    a = A[b + k, c]
                    w_ = B[b + k, c]
                    fe = h[j] + a
                    fw = h[j] + w_
                    so = face[j]
                    no = face[j - 1]
                    cu = a * (ve[j + 1] - ve[j - 1]) - w_ * (vw[j + 1] - vw[j - 1]) + 0.5 * (q[j + 1] - q[j - 1])
                    cv = 0.5 * (a * (ue[j + 1] - ue[j - 1]) - w_ * (uw[j + 1] - uw[j - 1])) + (r[j + 1] - r[j - 1])
                    tu = fe * ue[j] + fw * uw[j]
                    su = so * u[j + 1] + no * u[j - 1]
                    tv = fe * ve[j] + fw * vw[j]
                    sv = so * v[j + 1] + no * v[j - 1]
                    new_u[k][c] = IU[b + k, c] * (fu_ref[b + k, c] + 4.0 * tu + su + cu)
                    new_v[k][c] = IV[b + k, c] * (fv_ref[b + k, c] + tv + 4.0 * sv + cv)
            for k in range(UNROLL):
                put(dst, b + k, jnp.stack(new_u[k]), jnp.stack(new_v[k]))

        wrap(dst)

    zero = (U0, UE0, UW0, V0, VE0, VW0)
    one = (U1, UE1, UW1, V1, VE1, VW1)
    faces(True, None, one)
    sweep(one, zero, FU, FV)
    for _ in range(1, PIC):
        faces(False, zero, None)
        sweep(zero, one, FU, FV)
        sweep(one, zero, FU, FV)

    @pl.loop(0, STRIP)
    def _(i):
        u = U0[i + 1]
        v = V0[i + 1]
        FU[i] = u
        FV[i] = v
        mu = u - OU[i]
        mv = v - OV[i]
        OU[i] = mu
        OV[i] = mv
        put(one, i, IU[i] * mu, IV[i] * mv)

    wrap(one)
    for out, ref in ((out_u, FU), (out_v, FV)):
        @pl.loop(0, STRIP)
        def _(i):
            for c in range(2):
                nat[c, pl.ds(i, 8, stride=STRIP), :] = ref[i, c]

        for c in range(2):
            out[:, pl.ds(c * 128, 128)] = nat[c, pl.ds(HALO, TILE)]

    src, dst = one, zero
    for _ in range(1, ADJ):
        sweep(src, dst, OU, OV)
        src, dst = dst, src

    @pl.loop(0, STRIP)
    def _(i):
        T[i] = -FR[i] * (FU[i] * src[0][i + 1] + FV[i] * src[3][i + 1])

    cells = jnp.concatenate([T[:, 0].reshape(EXT, 128), T[:, 1].reshape(EXT, 128)], axis=1)
    fold = hot(TILE, 128, lambda r, c: r // 4 == c % 64)
    cols = mul(cells, fold)
    parts = []
    for par in range(2):
        pick = hot(32, EXT, lambda r, c: ((c % 8) * STRIP + c // 8) // 4 - HALO // 4 == 2 * r + par)
        parts.append(mul(pick, cols))
    lanes = lax.broadcasted_iota(jnp.int32, (32, 128), 1)
    grad[...] = jnp.where(lanes < 64, parts[0], parts[1])


def reduce_kernel(
    blk, grad, out,
    tiles, part, slots, red, rows,
    a_send, a_recv, b_send, b_recv, c_send, c_recv,
):
    gx = lax.axis_index("gx")
    gy = lax.axis_index("gy")

    def dev(dy, dx):
        return (lax.rem(gx + dx + GX, GX), lax.rem(gy + dy + GY, GY))

    def remote(src, dst, ss, rs, to):
        return pltpu.make_async_remote_copy(
            src_ref=src, dst_ref=dst, send_sem=ss, recv_sem=rs, device_id=to, device_id_type=MESH
        )

    barrier = pltpu.get_barrier_semaphore()
    peers = [(dy, 0) for dy in range(1, GY)] + [(0, dx) for dx in range(1, GX)]
    for dy, dx in peers:
        pl.semaphore_signal(barrier, inc=1, device_id=dev(dy, dx), device_id_type=MESH)
    pl.semaphore_wait(barrier, len(peers))

    first = [
        remote(grad, tiles.at[off], a_send.at[off], a_recv.at[off], dev(off, 0)) for off in range(1, GY)
    ]
    for c in first:
        c.start()
    tiles[0] = grad[...]
    for c in first:
        c.wait_recv()
    for k in range(4):
        total = jnp.zeros((32, 128), F32)
        for off in range(GY):
            owner = blk[lax.rem(gy - off + GY, GY), gx]
            total = total + jnp.where(owner == 4 * gy + k, tiles[off], 0.0)
        for g in range(GX):
            part[g, pl.ds(4 * k, 4)] = total[4 * g:4 * g + 4]
    second = []
    for off in range(1, GX):
        to = lax.rem(gx + off, GX)
        second.append(remote(part.at[to], slots.at[off], b_send.at[off], b_recv.at[off], dev(0, off)))
    for c in second:
        c.start()
    for c in second:
        c.wait_recv()
    total = part[gx]
    for off in range(1, GX):
        total = total + slots[off]
    red[...] = total
    third = [
        remote(red, rows.at[gx], c_send.at[off], c_recv.at[off], dev(0, off)) for off in range(1, GX)
    ]
    for c in third:
        c.start()
    rows[gx] = total
    for c in third:
        c.wait()
    for c in first + second:
        c.wait_send()
    for g in range(GX):
        for k in range(4):
            out[k, pl.ds(4 * g, 4)] = rows[g, pl.ds(4 * k, 4)]


def vmem(n=None):
    return pl.BlockSpec(memory_space=pltpu.VMEM)


def smem():
    return pl.BlockSpec(memory_space=pltpu.SMEM)


def per_device(thickness, driving, observed, control, ice_mask, tile_block):
    shape = jax.ShapeDtypeStruct
    blocks = tile_block.reshape(GY, GX)
    coarse_in = control.reshape(4, 32, 128)
    dma = pltpu.SemaphoreType.DMA
    h_north, h_south, h_west, h_east, coarse = pl.pallas_call(
        exchange_kernel,
        name="exchange",
        out_shape=(
            shape((5, HALO, TILE), F32),
            shape((5, HALO, TILE), F32),
            shape((EXT, 128), F32),
            shape((EXT, 128), F32),
            shape((9, 32, 128), F32),
        ),
        in_specs=[smem()] + [vmem()] * 4,
        out_specs=[vmem()] * 5,
        scratch_shapes=[
            pltpu.VMEM((TILE, 128), F32),
            pltpu.VMEM((TILE, 128), F32),
            pltpu.VMEM((GY, 32, 128), F32),
            pltpu.VMEM((GY, 32, 128), F32),
            dma((GY,)), dma((GY,)), dma((12,)), dma((12,)), dma((9,)), dma((9,)),
        ],
        compiler_params=pltpu.CompilerParams(collective_id=0, has_side_effects=True),
    )(blocks, thickness, driving, observed, coarse_in)

    field = pltpu.VMEM((STRIP, LT, 8, 128), F32)
    padded = pltpu.VMEM((STRIP + 2, LT, 8, 128), F32)
    vel_u, vel_v, grad = pl.pallas_call(
        solve_kernel,
        name="solve",
        out_shape=(shape((TILE, TILE), F32), shape((TILE, TILE), F32), shape((32, 128), F32)),
        in_specs=[smem()] + [vmem()] * 8,
        out_specs=[vmem()] * 3,
        scratch_shapes=[
            pltpu.VMEM((LT, EXT, 128), F32),
            pltpu.VMEM((3, 40, 128), F32),
            field, field, field, field, field, field, field,
            padded, field, field, field, field,
        ] + [padded] * 12,
        compiler_params=pltpu.CompilerParams(vmem_limit_bytes=40 << 20),
    )(ice_mask, thickness, driving, observed, h_north, h_south, h_west, h_east, coarse)

    total = pl.pallas_call(
        reduce_kernel,
        name="reduce",
        out_shape=shape((4, 32, 128), F32),
        in_specs=[smem(), vmem()],
        out_specs=vmem(),
        scratch_shapes=[
            pltpu.VMEM((GY, 32, 128), F32),
            pltpu.VMEM((GX, 16, 128), F32),
            pltpu.VMEM((GX, 16, 128), F32),
            pltpu.VMEM((16, 128), F32),
            pltpu.VMEM((GX, 16, 128), F32),
            dma((GY,)), dma((GY,)), dma((GX,)), dma((GX,)), dma((GX,)), dma((GX,)),
        ],
        compiler_params=pltpu.CompilerParams(collective_id=1, has_side_effects=True),
    )(blocks, grad)
    return vel_u, vel_v, total.reshape(4, 4096)


def solution(mesh):
    return jax.shard_map(
        per_device,
        mesh=mesh,
        in_specs=(P("gy", "gx"), P(None, "gy", "gx"), P(None, "gy", "gx"), P("gy", None), P(), P()),
        out_specs=(P("gy", "gx"), P("gy", "gx"), P("gy", None)),
        check_vma=False,
    )
```

```python
import jax
import jax.numpy as jnp
import numpy as np
from jax import lax
from jax.experimental import pallas as pl
from jax.experimental.pallas import tpu as pltpu
from jax.sharding import PartitionSpec as P

TILE = 256
HALO = 16
EXT = TILE + 2 * HALO
STRIP = EXT // 8
GROUP = STRIP // 4
LT = 3
PIC = 4
ADJ = 6
GX = 8
GY = 16
ROWS = 12
MROWS = 12
REMOTE = True
MESH = pl.DeviceIdType.MESH
F32 = jnp.float32

visc_scale = 0.1
strain_floor = 0.05


def kernel(
    blk, ice_ref, thick, drv, obs, ctl,
    out_u, out_v, out_g,
    nat, pack_w, pack_e, h_west, h_east, c_send, c_recv, coarse, cext,
    T, FU, FV, OU, OV, FR, IC, H, A, B, IU, IV,
    U0, UE0, UW0, V0, VE0, VW0, U1, UE1, UW1, V1, VE1, VW1,
    small, grad, tiles, part, slots, red, gathered,
    l_sem, o_sem, g_send, g_recv, x_send, x_recv, n_send, n_recv,
    a_send, a_recv, b_send, b_recv, d_send, d_recv,
):
    gx = lax.axis_index("gx")
    gy = lax.axis_index("gy")

    def dev(dy, dx):
        return (lax.rem(gx + dx + GX, GX), lax.rem(gy + dy + GY, GY))

    def remote(src, dst, ss, rs, to):
        return pltpu.make_async_remote_copy(
            src_ref=src, dst_ref=dst, send_sem=ss, recv_sem=rs, device_id=to, device_id_type=MESH
        )

    near = [(dy, dx) for dy in (-1, 0, 1) for dx in (-1, 0, 1) if (dy, dx) != (0, 0)]
    if REMOTE:
        barrier = pltpu.get_barrier_semaphore()
        peers = [(dy, 0) for dy in range(1, GY)] + [(0, dx) for dx in range(1, GX)]
        peers += [(dy, dx) for dy, dx in near if dy * dx]
        for dy, dx in peers:
            pl.semaphore_signal(barrier, inc=1, device_id=dev(dy, dx), device_id_type=MESH)

    inner = pl.ds(HALO, TILE)
    loads = []
    for f, src in enumerate((thick, drv.at[0], drv.at[1], obs.at[0], obs.at[1])):
        for c in range(2):
            loads.append(
                pltpu.make_async_copy(src.at[:, pl.ds(c * 128, 128)], nat.at[f, c, inner], l_sem.at[f, c])
            )
    for copy in loads:
        copy.start()

    for off in range(GY):
        c_send[off] = ctl[lax.rem(blk[lax.rem(gy + off, GY), gx], 4)]
    c_recv[0] = c_send[0]

    lane = lax.broadcasted_iota(jnp.int32, (8, 128), 1)
    sub = lax.broadcasted_iota(jnp.int32, (8, 128), 0)
    lane3 = lax.broadcasted_iota(jnp.int32, (LT, 8, 128), 2)

    gathers, halos, spread = [], [], []
    if REMOTE:
        pl.semaphore_wait(barrier, len(peers))
        gathers = [
            remote(c_send.at[off], c_recv.at[off], g_send.at[off], g_recv.at[off], dev(off, 0))
            for off in range(1, GY)
        ]
        for g in gathers:
            g.start()
    for copy in loads:
        copy.wait()
    if REMOTE:
        moves = [
            (nat.at[:, :, pl.ds(TILE, HALO)], nat.at[:, :, pl.ds(0, HALO)], (1, 0)),
            (nat.at[:, :, pl.ds(HALO, HALO)], nat.at[:, :, pl.ds(HALO + TILE, HALO)], (-1, 0)),
        ]
        halos = [remote(s, d, x_send.at[n], x_recv.at[n], dev(*to)) for n, (s, d, to) in enumerate(moves)]
        for h in halos:
            h.start()

    @pl.loop(0, TILE // 32)
    def _(t):
        for k in range(4):
            rows = pl.ds(pl.multiple_of(t * 32, 32) + 8 * k, 8)
            src = pl.ds(pl.multiple_of(t * 32, 32) + 8 * k + HALO, 8)
            w = nat[0, 0, src]
            e = nat[0, 1, src]
            for f in range(1, 5):
                w = jnp.where(lane < 16 * f, w, pltpu.roll(nat[f, 0, src], 16 * f, 1))
                e = jnp.where(lane >= 128 - 16 * f, e, pltpu.roll(nat[f, 1, src], 128 - 16 * f, 1))
            pack_w[rows, :] = w
            pack_e[rows, :] = e

    if REMOTE:
        lo, hi = pl.ds(0, HALO), pl.ds(TILE - HALO, HALO)
        first, last = pl.ds(0, HALO), pl.ds(TILE + HALO, HALO)
        moves = [
            (pack_e, h_west.at[inner], (0, 1)),
            (pack_w, h_east.at[inner], (0, -1)),
            (pack_e.at[hi], h_west.at[first], (1, 1)),
            (pack_e.at[lo], h_west.at[last], (-1, 1)),
            (pack_w.at[hi], h_east.at[first], (1, -1)),
            (pack_w.at[lo], h_east.at[last], (-1, -1)),
        ]
        sides = [
            remote(s, d, x_send.at[n + 2], x_recv.at[n + 2], dev(*to)) for n, (s, d, to) in enumerate(moves)
        ]
        for h in sides:
            h.start()
        halos = halos + sides
        for g in gathers:
            g.wait_recv()
    coarse[4] = c_recv[lax.rem(gy - blk[gy, gx] // 4 + GY, GY)]
    if REMOTE:
        for dy, dx in near:
            slot = (1 - dy) * 3 + (1 - dx)
            spread.append(remote(coarse.at[4], coarse.at[slot], n_send.at[slot], n_recv.at[slot], dev(dy, dx)))
        for n in spread:
            n.start()

    inside, iced = {}, {}
    for dy, dx in near + [(0, 0)]:
        ok = (gy + dy >= 0) & (gy + dy < GY) & (gx + dx >= 0) & (gx + dx < GX)
        flag = jnp.where(ok, 1.0, 0.0)
        at = ice_ref[jnp.clip(gy + dy, 0, GY - 1), jnp.clip(gx + dx, 0, GX - 1)]
        inside[dy, dx] = flag
        iced[dy, dx] = flag * at.astype(F32)

    def region(cls, table):
        def by_row(dx):
            mid = jnp.full((8, 128), table[0, dx], F32)
            if cls == 0:
                return jnp.where(sub == 0, table[-1, dx], mid)
            if cls == 2:
                return jnp.where(sub == 7, table[1, dx], mid)
            return mid

        center = by_row(0)
        edge = jnp.where(lane < HALO, by_row(1), jnp.where(lane >= 128 - HALO, by_row(-1), 0.0))
        return jnp.stack([center, center, edge])

    for cls in range(3):
        IC[cls] = region(cls, iced)

    def west(x):
        y = pltpu.roll(x, 1, 2)
        return jnp.where(lane3 == 0, jnp.concatenate([y[2:], y[:2]], axis=0), y)

    def east(x):
        y = pltpu.roll(x, 127, 2)
        return jnp.where(lane3 == 127, jnp.concatenate([y[1:], y[:1]], axis=0), y)

    def wrap(refs):
        for ref in refs:
            ref[0] = pltpu.roll(ref[STRIP], 1, 1)
            ref[STRIP + 1] = pltpu.roll(ref[1], 7, 1)

    for h in halos:
        h.wait()

    keep = [region(cls, inside) for cls in range(3)]
    for i in range(STRIP):
        at = pl.ds(i, 8, stride=STRIP)
        right = h_east[at, :]
        left = h_west[at, :]
        cls = 0 if i < 16 else (1 if i < 20 else 2)
        for f, dst in enumerate((T, FU, FV, OU, OV)):
            r = pltpu.roll(right, 128 - 16 * f, 1) if f else right
            l = pltpu.roll(left, 16 * f, 1) if f else left
            edge = jnp.where(lane < HALO, r, jnp.where(lane >= 128 - HALO, l, 0.0))
            x = jnp.stack([nat[f, 0, at, :], nat[f, 1, at, :], edge])
            if f == 0:
                x = jnp.where(keep[cls] > 0.0, x, 0.0)
            dst[i] = x

    for n in spread:
        n.wait_recv()
    for g, dx in enumerate((0, 1, -1)):
        flat = jnp.concatenate(
            [coarse[1 + dx, pl.ds(24, 8)], coarse[4 + dx], coarse[7 + dx, pl.ds(0, 8)]], axis=0
        )
        flat = jnp.exp(flat)
        cext[g, pl.ds(0, 48, stride=2), :] = flat
        cext[g, pl.ds(1, 48, stride=2), :] = pltpu.roll(flat, 64, 1)
    quarter = lane // 4
    for i in range(GROUP):
        at = pl.ds(12 + i, 8, stride=GROUP)
        mid, right, left = (cext[g, at, :] for g in range(3))
        edges = jnp.where(lane < 64, right, pltpu.roll(left, 64, 1))
        t0 = jnp.take_along_axis(mid, quarter, axis=1)
        t1 = jnp.take_along_axis(mid, quarter + 32, axis=1)
        t2 = jnp.take_along_axis(edges, jnp.where(lane < 64, quarter, 96 + quarter), axis=1)
        FR[i] = jnp.stack([t0, t1, t2])

    base = float(visc_scale * np.power(strain_floor, -1.0 / 3.0))

    def put(dst, i, u, v):
        U, UE, UW, V, VE, VW = dst
        U[i + 1] = u
        UE[i + 1] = east(u)
        UW[i + 1] = west(u)
        V[i + 1] = v
        VE[i + 1] = east(v)
        VW[i + 1] = west(v)

    def viscosity(src):
        @pl.loop(0, STRIP // MROWS)
        def _(it):
            for k in range(MROWS):
                i = it * MROWS + k
                if src is None:
                    m = (0.5 * base) * T[i]
                else:
                    U, UE, UW, V, VE, VW = src
                    ux = 0.5 * (UE[i + 1] - UW[i + 1])
                    vx = 0.5 * (VE[i + 1] - VW[i + 1])
                    uy = 0.5 * (U[i + 2] - U[i])
                    vy = 0.5 * (V[i + 2] - V[i])
                    sh = uy + vx
                    strain = ux * ux + vy * vy + ux * vy + 0.25 * (sh * sh) + strain_floor
                    m = (0.5 * visc_scale) * T[i] * jnp.exp2(jnp.log2(strain) * (-1.0 / 3.0))
                H[i + 1] = m
                A[i] = east(m)
                B[i] = west(m)

        wrap([H])

    def sweep(src, dst, fu_ref, fv_ref, fresh):
        @pl.loop(0, STRIP // ROWS)
        def _(it):
            b = it * ROWS
            new_u = [[None] * LT for _ in range(ROWS)]
            new_v = [[None] * LT for _ in range(ROWS)]
            n = ROWS + 2
            for c in range(LT):
                h = [H[b + j, c] for j in range(n)]
                face = [h[j] + h[j + 1] for j in range(n - 1)]
                if src is not None:
                    u, ue, uw, v, ve, vw = ([ref[b + j, c] for j in range(n)] for ref in src)
                    q = [h[j] * (ve[j] - vw[j]) for j in range(n)]
                    r = [h[j] * (ue[j] - uw[j]) for j in range(n)]
                for k in range(ROWS):
                    j = k + 1
                    i = b + k
                    a = A[i, c]
                    w_ = B[i, c]
                    fe = h[j] + a
                    fw = h[j] + w_
                    so = face[j]
                    no = face[j - 1]
                    if fresh:
                        ew = fe + fw
                        sn = so + no
                        fr = FR[it * (ROWS // 4) + k // 4, c]
                        step = i // 4
                        cls = jnp.where(step < 4, 0, jnp.where(step < 5, 1, 2))
                        ice = IC[cls, c]
                        if c == 2:
                            fr = jnp.where(ice > 0.0, fr, 1.0)
                        iu = ice / (fr + 4.0 * ew + sn)
                        iv = ice / (fr + ew + 4.0 * sn)
                        IU[i, c] = iu
                        IV[i, c] = iv
                    else:
                        iu = IU[i, c]
                        iv = IV[i, c]
                    fu = fu_ref[i, c]
                    fv = fv_ref[i, c]
                    if src is not None:
                        cu = a * (ve[j + 1] - ve[j - 1]) - w_ * (vw[j + 1] - vw[j - 1]) + 0.5 * (q[j + 1] - q[j - 1])
                        cv = 0.5 * (a * (ue[j + 1] - ue[j - 1]) - w_ * (uw[j + 1] - uw[j - 1])) + (r[j + 1] - r[j - 1])
                        tu = fe * ue[j] + fw * uw[j]
                        su = so * u[j + 1] + no * u[j - 1]
                        tv = fe * ve[j] + fw * vw[j]
                        sv = so * v[j + 1] + no * v[j - 1]
                        fu = fu + 4.0 * tu + su + cu
                        fv = fv + tv + 4.0 * sv + cv
                    new_u[k][c] = iu * fu
                    new_v[k][c] = iv * fv
            for k in range(ROWS):
                put(dst, b + k, jnp.stack(new_u[k]), jnp.stack(new_v[k]))

        wrap(dst)

    zero = (U0, UE0, UW0, V0, VE0, VW0)
    one = (U1, UE1, UW1, V1, VE1, VW1)
    viscosity(None)
    sweep(None, one, FU, FV, True)
    sweep(one, zero, FU, FV, False)

    @pl.loop(1, PIC)
    def _(_):
        viscosity(zero)
        sweep(zero, one, FU, FV, True)
        sweep(one, zero, FU, FV, False)

    @pl.loop(0, STRIP // 4)
    def _(it):
        for k in range(4):
            i = it * 4 + k
            u = U0[i + 1]
            v = V0[i + 1]
            FU[i] = u
            FV[i] = v
            at = pl.ds(i, 8, stride=STRIP)
            for c in range(2):
                nat[0, c, at, :] = u[c]
                nat[1, c, at, :] = v[c]
            mu = u - OU[i]
            mv = v - OV[i]
            OU[i] = mu
            OV[i] = mv
            put(one, i, IU[i] * mu, IV[i] * mv)

    stores = []
    for f, dst in enumerate((out_u, out_v)):
        for c in range(2):
            stores.append(
                pltpu.make_async_copy(nat.at[f, c, inner], dst.at[:, pl.ds(c * 128, 128)], o_sem.at[f, c])
            )
    for s in stores:
        s.start()
    wrap(one)

    @pl.loop(0, (ADJ - 2) // 2)
    def _(_):
        sweep(one, zero, OU, OV, False)
        sweep(zero, one, OU, OV, False)

    sweep(one, zero, OU, OV, False)

    for i in range(GROUP):
        total = None
        for k in range(4):
            j = i * 4 + k
            cell = [FU[j, c] * U0[j + 1, c] + FV[j, c] * V0[j + 1, c] for c in range(2)]
            total = cell if total is None else [total[c] + cell[c] for c in range(2)]
        spots = []
        for c in range(2):
            x = -FR[i, c] * total[c]
            x = x + pltpu.roll(x, 127, 1)
            x = x + pltpu.roll(x, 126, 1)
            spots.append(jnp.take_along_axis(x, (lane % 32) * 4, axis=1))
        both = jnp.where(lane % 64 < 32, spots[0], spots[1])
        small[pl.ds(i, 8, stride=GROUP), :] = both
    even = small[pl.ds(4, 32, stride=2), :]
    odd = small[pl.ds(5, 32, stride=2), :]
    wide = lax.broadcasted_iota(jnp.int32, (32, 128), 1)
    grad[...] = jnp.where(wide < 64, even, odd)

    first, second, third = [], [], []
    if REMOTE:
        first = [
            remote(grad, tiles.at[off], a_send.at[off], a_recv.at[off], dev(off, 0)) for off in range(1, GY)
        ]
    for c in first:
        c.start()
    tiles[0] = grad[...]
    for c in first:
        c.wait_recv()
    for k in range(4):
        total = jnp.zeros((32, 128), F32)
        for off in range(GY):
            owner = blk[lax.rem(gy - off + GY, GY), gx]
            total = total + jnp.where(owner == 4 * gy + k, tiles[off], 0.0)
        for g in range(GX):
            part[g, pl.ds(4 * k, 4)] = total[4 * g:4 * g + 4]
    if REMOTE:
        for off in range(1, GX):
            to = lax.rem(gx + off, GX)
            second.append(remote(part.at[to], slots.at[off], b_send.at[off], b_recv.at[off], dev(0, off)))
    for c in second:
        c.start()
    for c in second:
        c.wait_recv()
    total = part[gx]
    for off in range(1, GX):
        total = total + slots[off]
    red[...] = total
    if REMOTE:
        third = [
            remote(red, gathered.at[gx], d_send.at[off], d_recv.at[off], dev(0, off)) for off in range(1, GX)
        ]
    for c in third:
        c.start()
    gathered[gx] = total
    for c in third:
        c.wait()
    for g in range(GX):
        for k in range(4):
            out_g[k, pl.ds(4 * g, 4)] = gathered[g, pl.ds(4 * k, 4)]
    for c in gathers + spread + first + second:
        c.wait_send()
    for s in stores:
        s.wait()


def call(*operands):
    shape = jax.ShapeDtypeStruct
    dma = pltpu.SemaphoreType.DMA
    anywhere = pl.BlockSpec(memory_space=pl.ANY)
    smem = pl.BlockSpec(memory_space=pltpu.SMEM)
    vmem = pl.BlockSpec(memory_space=pltpu.VMEM)
    field = pltpu.VMEM((STRIP, LT, 8, 128), F32)
    padded = pltpu.VMEM((STRIP + 2, LT, 8, 128), F32)
    flat = pltpu.VMEM((32, 128), F32)
    return pl.pallas_call(
        kernel,
        name="friction_gradient",
        out_shape=(shape((TILE, TILE), F32), shape((TILE, TILE), F32), shape((4, 32, 128), F32)),
        in_specs=[smem, smem, anywhere, anywhere, anywhere, vmem],
        out_specs=[anywhere, anywhere, vmem],
        scratch_shapes=[
            pltpu.VMEM((5, 2, EXT, 128), F32),
            pltpu.VMEM((TILE, 128), F32),
            pltpu.VMEM((TILE, 128), F32),
            pltpu.VMEM((EXT, 128), F32),
            pltpu.VMEM((EXT, 128), F32),
            pltpu.VMEM((GY, 32, 128), F32),
            pltpu.VMEM((GY, 32, 128), F32),
            pltpu.VMEM((9, 32, 128), F32),
            pltpu.VMEM((3, 96, 128), F32),
            field, field, field, field, field,
            pltpu.VMEM((GROUP, LT, 8, 128), F32),
            pltpu.VMEM((3, LT, 8, 128), F32),
            padded, field, field, field, field,
        ] + [padded] * 12 + [
            pltpu.VMEM((72, 128), F32),
            flat,
            pltpu.VMEM((GY, 32, 128), F32),
            pltpu.VMEM((GX, 16, 128), F32),
            pltpu.VMEM((GX, 16, 128), F32),
            pltpu.VMEM((16, 128), F32),
            pltpu.VMEM((GX, 16, 128), F32),
            dma((5, 2)), dma((2, 2)),
            dma((GY,)), dma((GY,)), dma((8,)), dma((8,)), dma((9,)), dma((9,)),
            dma((GY,)), dma((GY,)), dma((GX,)), dma((GX,)), dma((GX,)), dma((GX,)),
        ],
        compiler_params=pltpu.CompilerParams(
            vmem_limit_bytes=48 << 20,
            **(dict(collective_id=0, has_side_effects=True) if REMOTE else {}),
        ),
    )(*operands)


def per_device(thickness, driving, observed, control, ice_mask, tile_block):
    vel_u, vel_v, total = call(
        tile_block.reshape(GY, GX), ice_mask, thickness, driving, observed, control.reshape(4, 32, 128)
    )
    return vel_u, vel_v, total.reshape(4, 4096)


def solution(mesh):
    return jax.shard_map(
        per_device,
        mesh=mesh,
        in_specs=(P("gy", "gx"), P(None, "gy", "gx"), P(None, "gy", "gx"), P("gy", None), P(), P()),
        out_specs=(P("gy", "gx"), P("gy", "gx"), P("gy", None)),
        check_vma=False,
    )
```

```python
import jax
import jax.numpy as jnp
import numpy as np
from jax import lax
from jax.experimental import pallas as pl
from jax.experimental.pallas import tpu as pltpu
from jax.sharding import PartitionSpec as P

TILE = 256
HALO = 16
EXT = TILE + 2 * HALO
STRIP = EXT // 8
GROUP = STRIP // 4
LT = 3
PIC = 4
ADJ = 6
GX = 8
GY = 16
ROWS = 36
MROWS = 36
REMOTE = True
MESH = pl.DeviceIdType.MESH
F32 = jnp.float32

visc_scale = 0.1
strain_floor = 0.05


def kernel(
    blk, ice_ref, thick, drv, obs, ctl,
    out_u, out_v, out_g,
    nat, pack_w, pack_e, h_west, h_east, c_in, c_own, c_send, c_recv, coarse, cext,
    T, FU, FV, OU, OV, FR, IC, H, A, B, IU, IV,
    U0, UE0, UW0, V0, VE0, VW0, U1, UE1, UW1, V1, VE1, VW1,
    small, grad, sums, tiles, part, slots, red, gathered,
    k_sem, l_sem, o_sem, g_send, g_recv, x_send, x_recv, n_send, n_recv,
    a_send, a_recv, b_send, b_recv, d_send, d_recv,
):
    gx = lax.axis_index("gx")
    gy = lax.axis_index("gy")

    def dev(dy, dx):
        return (lax.rem(gx + dx + GX, GX), lax.rem(gy + dy + GY, GY))

    def remote(src, dst, ss, rs, to):
        return pltpu.make_async_remote_copy(
            src_ref=src, dst_ref=dst, send_sem=ss, recv_sem=rs, device_id=to, device_id_type=MESH
        )

    near = [(dy, dx) for dy in (-1, 0, 1) for dx in (-1, 0, 1) if (dy, dx) != (0, 0)]
    if REMOTE:
        barrier = pltpu.get_barrier_semaphore()
        peers = [(dy, 0) for dy in range(1, GY)] + [(0, dx) for dx in range(1, GX)]
        peers += [(dy, dx) for dy, dx in near if dy * dx]
        for dy, dx in peers:
            pl.semaphore_signal(barrier, inc=1, device_id=dev(dy, dx), device_id_type=MESH)

    rates = pltpu.make_async_copy(ctl, c_in, k_sem)
    rates.start()

    inner = pl.ds(HALO, TILE)
    loads = []
    for f, src in enumerate((thick, drv.at[0], drv.at[1], obs.at[0], obs.at[1])):
        for c in range(2):
            loads.append(
                pltpu.make_async_copy(src.at[:, pl.ds(c * 128, 128)], nat.at[f, c, inner], l_sem.at[f, c])
            )
    for copy in loads:
        copy.start()

    lane = lax.broadcasted_iota(jnp.int32, (8, 128), 1)
    sub = lax.broadcasted_iota(jnp.int32, (8, 128), 0)
    lane3 = lax.broadcasted_iota(jnp.int32, (LT, 8, 128), 2)

    rates.wait()
    for t in range(32):
        x = c_in[:, pl.ds(t * 128, 128)]
        for k in range(4):
            c_own[k, pl.ds(t, 1)] = x[k:k + 1]
    for off in range(GY):
        c_send[off] = c_own[lax.rem(blk[gx, 0, lax.rem(gy + off, GY)], 4)]
    c_recv[0] = c_send[0]

    for f in (3, 4):
        for c in range(2):
            nat[f, c, pl.ds(0, 8)] = jnp.zeros((8, 128), F32)
            nat[f, c, pl.ds(EXT - 8, 8)] = jnp.zeros((8, 128), F32)
    for copy in loads:
        copy.wait()
    shifts = (0, 16, 32, 48, 56)
    for t in range(16):
        w = e = None
        for half in range(2):
            at = pl.ds(HALO + half * 128 + t * 8, 8)
            for f in range(5):
                shift = shifts[f] + 64 * half
                x = nat[f, 0, at]
                y = nat[f, 1, at]
                if shift:
                    x = pltpu.roll(x, shift, 1)
                    y = pltpu.roll(y, 128 - shift, 1)
                w = x if w is None else jnp.where(lane < shift, w, x)
                e = y if e is None else jnp.where(lane >= 128 - shift, e, y)
        pack_w[pl.ds(t * 8, 8), :] = w
        pack_e[pl.ds(t * 8, 8), :] = e

    gathers, halos, spread = [], [], []
    if REMOTE:
        pl.semaphore_wait(barrier, len(peers))
        gathers = [
            remote(c_send.at[off], c_recv.at[off], g_send.at[off], g_recv.at[off], dev(off, 0))
            for off in range(1, GY)
        ]
        main, obs2 = pl.ds(0, 3), pl.ds(3, 2)
        half = pl.ds(HALO, 128)
        head, tail = pl.ds(0, HALO), pl.ds(112, HALO)
        first, last = pl.ds(0, HALO), pl.ds(TILE + HALO, HALO)
        moves = [
            (pack_e, h_west.at[half], (0, 1)),
            (pack_w, h_east.at[half], (0, -1)),
            (nat.at[main, :, pl.ds(TILE, HALO)], nat.at[main, :, first], (1, 0)),
            (nat.at[main, :, pl.ds(HALO, HALO)], nat.at[main, :, last], (-1, 0)),
            (pack_e.at[tail], h_west.at[first], (1, 1)),
            (pack_e.at[head], h_west.at[last], (-1, 1)),
            (pack_w.at[tail], h_east.at[first], (1, -1)),
            (pack_w.at[head], h_east.at[last], (-1, -1)),
            (nat.at[obs2, :, pl.ds(TILE + 8, 8)], nat.at[obs2, :, pl.ds(8, 8)], (1, 0)),
            (nat.at[obs2, :, pl.ds(HALO, 8)], nat.at[obs2, :, pl.ds(TILE + HALO, 8)], (-1, 0)),
        ]
        halos = [remote(s, d, x_send.at[n], x_recv.at[n], dev(*to)) for n, (s, d, to) in enumerate(moves)]
        for g in gathers + halos:
            g.start()
        for g in gathers:
            g.wait_recv()
    coarse[4] = c_recv[lax.rem(gy - blk[gx, 0, gy] // 4 + GY, GY)]
    if REMOTE:
        for dy, dx in near:
            slot = (1 - dy) * 3 + (1 - dx)
            rows = (pl.ds(0, 8), pl.ds(0, 32), pl.ds(24, 8))[dy + 1]
            spread.append(
                remote(coarse.at[4, rows], coarse.at[slot, rows], n_send.at[slot], n_recv.at[slot], dev(dy, dx))
            )
        for n in spread:
            n.start()

    inside, iced = {}, {}
    for dy, dx in near + [(0, 0)]:
        ok = (gy + dy >= 0) & (gy + dy < GY) & (gx + dx >= 0) & (gx + dx < GX)
        flag = jnp.where(ok, 1.0, 0.0)
        at = ice_ref[jnp.clip(gx + dx, 0, GX - 1), jnp.clip(gy + dy, 0, GY - 1)]
        inside[dy, dx] = flag
        iced[dy, dx] = flag * at.astype(F32)

    def region(cls, table):
        def by_row(dx):
            mid = jnp.full((8, 128), table[0, dx], F32)
            if cls == 0:
                return jnp.where(sub == 0, table[-1, dx], mid)
            if cls == 2:
                return jnp.where(sub == 7, table[1, dx], mid)
            return mid

        center = by_row(0)
        edge = jnp.where(lane < HALO, by_row(1), jnp.where(lane >= 128 - HALO, by_row(-1), 0.0))
        return jnp.stack([center, center, edge])

    for cls in range(3):
        IC[cls] = region(cls, iced)

    def west(x):
        y = pltpu.roll(x, 1, 2)
        return jnp.where(lane3 == 0, jnp.concatenate([y[2:], y[:2]], axis=0), y)

    def east(x):
        y = pltpu.roll(x, 127, 2)
        return jnp.where(lane3 == 127, jnp.concatenate([y[1:], y[:1]], axis=0), y)

    def wrap(refs):
        for ref in refs:
            ref[0] = pltpu.roll(ref[STRIP], 1, 1)
            ref[STRIP + 1] = pltpu.roll(ref[1], 7, 1)

    for h in halos:
        h.wait()

    for ref in (h_west, h_east):
        ref[pl.ds(HALO + 128, 128)] = pltpu.roll(ref[pl.ds(HALO, 128)], 64, 1)
        ref[pl.ds(0, HALO)] = pltpu.roll(ref[pl.ds(0, HALO)], 64, 1)

    keep = [region(cls, inside) for cls in range(3)]
    for i in range(STRIP):
        at = pl.ds(i, 8, stride=STRIP)
        right = h_east[at, :]
        left = h_west[at, :]
        cls = 0 if i < 16 else (1 if i < 20 else 2)
        for f, dst in enumerate((T, FU, FV, OU, OV)):
            r = pltpu.roll(right, 128 - shifts[f], 1) if f else right
            l = pltpu.roll(left, shifts[f], 1) if f else left
            edge = jnp.where(lane < HALO, r, jnp.where(lane >= 128 - HALO, l, 0.0))
            x = jnp.stack([nat[f, 0, at, :], nat[f, 1, at, :], edge])
            if f == 0:
                x = jnp.where(keep[cls] > 0.0, x, 0.0)
            dst[i] = x

    base = float(visc_scale * np.power(strain_floor, -1.0 / 3.0))

    def put(dst, i, u, v):
        U, UE, UW, V, VE, VW = dst
        U[i + 1] = u
        UE[i + 1] = east(u)
        UW[i + 1] = west(u)
        V[i + 1] = v
        VE[i + 1] = east(v)
        VW[i + 1] = west(v)

    def viscosity(src):
        @pl.loop(0, STRIP // MROWS)
        def _(it):
            for k in range(MROWS):
                i = it * MROWS + k
                if src is None:
                    m = (0.5 * base) * T[i]
                else:
                    U, UE, UW, V, VE, VW = src
                    ux = 0.5 * (UE[i + 1] - UW[i + 1])
                    vx = 0.5 * (VE[i + 1] - VW[i + 1])
                    uy = 0.5 * (U[i + 2] - U[i])
                    vy = 0.5 * (V[i + 2] - V[i])
                    sh = uy + vx
                    strain = ux * ux + vy * vy + ux * vy + 0.25 * (sh * sh) + strain_floor
                    m = (0.5 * visc_scale) * T[i] * jnp.exp2(jnp.log2(strain) * (-1.0 / 3.0))
                H[i + 1] = m
                A[i] = east(m)
                B[i] = west(m)

        wrap([H])

    def sweep(src, dst, fu_ref, fv_ref, fresh):
        @pl.loop(0, STRIP // ROWS)
        def _(it):
            b = it * ROWS
            new_u = [[None] * LT for _ in range(ROWS)]
            new_v = [[None] * LT for _ in range(ROWS)]
            n = ROWS + 2
            for c in range(LT):
                h = [H[b + j, c] for j in range(n)]
                face = [h[j] + h[j + 1] for j in range(n - 1)]
                if src is not None:
                    u, ue, uw, v, ve, vw = ([ref[b + j, c] for j in range(n)] for ref in src)
                    q = [h[j] * (ve[j] - vw[j]) for j in range(n)]
                    r = [h[j] * (ue[j] - uw[j]) for j in range(n)]
                for k in range(ROWS):
                    j = k + 1
                    i = b + k
                    a = A[i, c]
                    w_ = B[i, c]
                    fe = h[j] + a
                    fw = h[j] + w_
                    so = face[j]
                    no = face[j - 1]
                    if fresh:
                        ew = fe + fw
                        sn = so + no
                        fr = FR[it * (ROWS // 4) + k // 4, c]
                        step = i // 4
                        cls = jnp.where(step < 4, 0, jnp.where(step < 5, 1, 2))
                        ice = IC[cls, c]
                        if c == 2:
                            fr = jnp.where(ice > 0.0, fr, 1.0)
                        iu = ice / (fr + 4.0 * ew + sn)
                        iv = ice / (fr + ew + 4.0 * sn)
                        IU[i, c] = iu
                        IV[i, c] = iv
                    else:
                        iu = IU[i, c]
                        iv = IV[i, c]
                    fu = fu_ref[i, c]
                    fv = fv_ref[i, c]
                    if src is not None:
                        cu = a * (ve[j + 1] - ve[j - 1]) - w_ * (vw[j + 1] - vw[j - 1]) + 0.5 * (q[j + 1] - q[j - 1])
                        cv = 0.5 * (a * (ue[j + 1] - ue[j - 1]) - w_ * (uw[j + 1] - uw[j - 1])) + (r[j + 1] - r[j - 1])
                        tu = fe * ue[j] + fw * uw[j]
                        su = so * u[j + 1] + no * u[j - 1]
                        tv = fe * ve[j] + fw * vw[j]
                        sv = so * v[j + 1] + no * v[j - 1]
                        fu = fu + 4.0 * tu + su + cu
                        fv = fv + tv + 4.0 * sv + cv
                    new_u[k][c] = iu * fu
                    new_v[k][c] = iv * fv
            for k in range(ROWS):
                put(dst, b + k, jnp.stack(new_u[k]), jnp.stack(new_v[k]))

        wrap(dst)

    zero = (U0, UE0, UW0, V0, VE0, VW0)
    one = (U1, UE1, UW1, V1, VE1, VW1)
    viscosity(None)

    for n in spread:
        n.wait_recv()
    for g, dx in enumerate((0, 1, -1)):
        flat = jnp.concatenate(
            [coarse[1 + dx, pl.ds(24, 8)], coarse[4 + dx], coarse[7 + dx, pl.ds(0, 8)]], axis=0
        )
        flat = jnp.exp(flat)
        cext[g, pl.ds(0, 48, stride=2), :] = flat
        cext[g, pl.ds(1, 48, stride=2), :] = pltpu.roll(flat, 64, 1)
    quarter = lane // 4
    for i in range(GROUP):
        at = pl.ds(12 + i, 8, stride=GROUP)
        mid, right, left = (cext[g, at, :] for g in range(3))
        edges = jnp.where(lane < 64, right, pltpu.roll(left, 64, 1))
        t0 = jnp.take_along_axis(mid, quarter, axis=1)
        t1 = jnp.take_along_axis(mid, quarter + 32, axis=1)
        t2 = jnp.take_along_axis(edges, jnp.where(lane < 64, quarter, 96 + quarter), axis=1)
        FR[i] = jnp.stack([t0, t1, t2])

    sweep(None, one, FU, FV, True)
    sweep(one, zero, FU, FV, False)

    @pl.loop(1, PIC)
    def _(_):
        viscosity(zero)
        sweep(zero, one, FU, FV, True)
        sweep(one, zero, FU, FV, False)

    @pl.loop(0, STRIP // 4)
    def _(it):
        for k in range(4):
            i = it * 4 + k
            u = U0[i + 1]
            v = V0[i + 1]
            FU[i] = u
            FV[i] = v
            at = pl.ds(i, 8, stride=STRIP)
            for c in range(2):
                nat[0, c, at, :] = u[c]
                nat[1, c, at, :] = v[c]
            mu = u - OU[i]
            mv = v - OV[i]
            OU[i] = mu
            OV[i] = mv
            put(one, i, IU[i] * mu, IV[i] * mv)

    stores = []
    for f, dst in enumerate((out_u, out_v)):
        for c in range(2):
            stores.append(
                pltpu.make_async_copy(nat.at[f, c, inner], dst.at[:, pl.ds(c * 128, 128)], o_sem.at[f, c])
            )
    for s in stores:
        s.start()
    wrap(one)

    @pl.loop(0, (ADJ - 2) // 2)
    def _(_):
        sweep(one, zero, OU, OV, False)
        sweep(zero, one, OU, OV, False)

    sweep(one, zero, OU, OV, False)

    for i in range(GROUP):
        total = None
        for k in range(4):
            j = i * 4 + k
            cell = [FU[j, c] * U0[j + 1, c] + FV[j, c] * V0[j + 1, c] for c in range(2)]
            total = cell if total is None else [total[c] + cell[c] for c in range(2)]
        spots = []
        for c in range(2):
            x = -FR[i, c] * total[c]
            x = x + pltpu.roll(x, 127, 1)
            x = x + pltpu.roll(x, 126, 1)
            spots.append(jnp.take_along_axis(x, (lane % 32) * 4, axis=1))
        both = jnp.where(lane % 64 < 32, spots[0], spots[1])
        small[pl.ds(i, 8, stride=GROUP), :] = both
    even = small[pl.ds(4, 32, stride=2), :]
    odd = small[pl.ds(5, 32, stride=2), :]
    wide = lax.broadcasted_iota(jnp.int32, (32, 128), 1)
    grad[...] = jnp.where(wide < 64, even, odd)

    first, second, third = [], [], []
    for g in range(GX):
        part[g] = grad[pl.ds(4 * g, 4), :]
    if REMOTE:
        first = [
            remote(part.at[lax.rem(gx + off, GX)], slots.at[off], b_send.at[off], b_recv.at[off], dev(0, off))
            for off in range(1, GX)
        ]
    for c in first:
        c.start()
    slots[0] = part[gx]
    owners = [blk[lax.rem(gx - off + GX, GX), 0, gy] for off in range(GX)]
    which = lax.broadcasted_iota(jnp.int32, (16, 128), 0) % 4
    for c in first:
        c.wait_recv()
    cells = []
    for t in range(GX):
        x = slots[t]
        cells.append(jnp.concatenate([jnp.broadcast_to(x[j:j + 1], (4, 128)) for j in range(4)], axis=0))
    if REMOTE:
        second = [
            remote(sums.at[off], tiles.at[off], a_send.at[off], a_recv.at[off], dev(off, 0)) for off in range(1, GY)
        ]
    for off in list(range(1, GY)) + [0]:
        lowest = 4 * lax.rem(gy + off, GY)
        total = jnp.zeros((16, 128), F32)
        for t in range(GX):
            total = total + jnp.where(which == owners[t] - lowest, cells[t], 0.0)
        sums[off] = total
        if off > 0 and REMOTE:
            second[off - 1].start()
    total = sums[0]
    for off in range(1, GY):
        if REMOTE:
            second[off - 1].wait_recv()
        total = total + tiles[off]
    red[...] = total
    if REMOTE:
        third = [
            remote(red, gathered.at[gx], d_send.at[off], d_recv.at[off], dev(0, off)) for off in range(1, GX)
        ]
    for c in third:
        c.start()
    gathered[gx] = total
    for c in third:
        c.wait()
    for g in range(GX):
        for j in range(4):
            out_g[:, pl.ds((4 * g + j) * 128, 128)] = gathered[g, pl.ds(4 * j, 4)]
    for c in gathers + spread + first + second:
        c.wait_send()
    for s in stores:
        s.wait()


def call(*operands):
    shape = jax.ShapeDtypeStruct
    dma = pltpu.SemaphoreType.DMA
    hbm = pl.BlockSpec(memory_space=pltpu.HBM)
    smem = pl.BlockSpec(memory_space=pltpu.SMEM)
    vmem = pl.BlockSpec(memory_space=pltpu.VMEM)
    field = pltpu.VMEM((STRIP, LT, 8, 128), F32)
    padded = pltpu.VMEM((STRIP + 2, LT, 8, 128), F32)
    flat = pltpu.VMEM((32, 128), F32)
    return pl.pallas_call(
        kernel,
        name="friction_gradient",
        out_shape=(shape((TILE, TILE), F32), shape((TILE, TILE), F32), shape((4, 4096), F32)),
        in_specs=[smem, smem, hbm, hbm, hbm, hbm],
        out_specs=[hbm, hbm, vmem],
        scratch_shapes=[
            pltpu.VMEM((5, 2, EXT, 128), F32),
            pltpu.VMEM((128, 128), F32),
            pltpu.VMEM((128, 128), F32),
            pltpu.VMEM((EXT, 128), F32),
            pltpu.VMEM((EXT, 128), F32),
            pltpu.VMEM((4, 4096), F32),
            pltpu.VMEM((4, 32, 128), F32),
            pltpu.VMEM((GY, 32, 128), F32),
            pltpu.VMEM((GY, 32, 128), F32),
            pltpu.VMEM((9, 32, 128), F32),
            pltpu.VMEM((3, 96, 128), F32),
            field, field, field, field, field,
            pltpu.VMEM((GROUP, LT, 8, 128), F32),
            pltpu.VMEM((3, LT, 8, 128), F32),
            padded, field, field, field, field,
        ] + [padded] * 12 + [
            pltpu.VMEM((72, 128), F32),
            flat,
            pltpu.VMEM((GY, 16, 128), F32),
            pltpu.VMEM((GY, 16, 128), F32),
            pltpu.VMEM((GX, 4, 128), F32),
            pltpu.VMEM((GX, 4, 128), F32),
            pltpu.VMEM((16, 128), F32),
            pltpu.VMEM((GX, 16, 128), F32),
            dma, dma((5, 2)), dma((2, 2)),
            dma((GY,)), dma((GY,)), dma((10,)), dma((10,)), dma((9,)), dma((9,)),
            dma((GY,)), dma((GY,)), dma((GX,)), dma((GX,)), dma((GX,)), dma((GX,)),
        ],
        compiler_params=pltpu.CompilerParams(
            vmem_limit_bytes=60 << 20,
            **(dict(collective_id=0, has_side_effects=True) if REMOTE else {}),
        ),
    )(*operands)


def per_device(thickness, driving, observed, control, ice_mask, tile_block):
    return call(
        tile_block.transpose(1, 2, 0), ice_mask.T, thickness, driving, observed, control
    )


def solution(mesh):
    return jax.shard_map(
        per_device,
        mesh=mesh,
        in_specs=(P("gy", "gx"), P(None, "gy", "gx"), P(None, "gy", "gx"), P("gy", None), P(), P()),
        out_specs=(P("gy", "gx"), P("gy", "gx"), P("gy", None)),
        check_vma=False,
    )
```

```python
import jax
import jax.numpy as jnp
import numpy as np
from jax import lax
from jax.experimental import pallas as pl
from jax.experimental.pallas import tpu as pltpu
from jax.sharding import PartitionSpec as P

TILE = 256
HALO = 16
EXT = TILE + 2 * HALO
STRIP = EXT // 8
GROUP = STRIP // 4
LT = 3
PIC = 4
ADJ = 6
GX = 8
GY = 16
ROWS = 36
MROWS = 36
REMOTE = True
MESH = pl.DeviceIdType.MESH
F32 = jnp.float32

visc_scale = 0.1
strain_floor = 0.05


def kernel(
    blk, ice_ref, thick, drv, obs, ctl,
    out_u, out_v, out_g,
    nat, pack_w, pack_e, h_west, h_east, c_in, c_own, c_side, c_ends, c_send, c_recv, coarse, cext,
    T, FU, FV, OU, OV, FR, IC, H, A, B, IU, IV,
    U0, UE0, UW0, V0, VE0, VW0, U1, UE1, UW1, V1, VE1, VW1,
    small, grad, sums, tiles, part, slots, red, gathered,
    k_sem, l_sem, o_sem, g_send, g_recv, x_send, x_recv,
    a_send, a_recv, b_send, b_recv, d_send, d_recv,
):
    gx = lax.axis_index("gx")
    gy = lax.axis_index("gy")

    def dev(dy, dx):
        return (lax.rem(gx + dx + GX, GX), lax.rem(gy + dy + GY, GY))

    def remote(src, dst, ss, rs, to):
        return pltpu.make_async_remote_copy(
            src_ref=src, dst_ref=dst, send_sem=ss, recv_sem=rs, device_id=to, device_id_type=MESH
        )

    rates = pltpu.make_async_copy(ctl, c_in, k_sem)
    rates.start()
    near = [(dy, dx) for dy in (-1, 0, 1) for dx in (-1, 0, 1) if (dy, dx) != (0, 0)]
    if REMOTE:
        barrier = pltpu.get_barrier_semaphore()
        peers = [(dy, 0) for dy in range(1, GY)] + [(0, dx) for dx in range(1, GX)]
        peers += [(dy, dx) for dy, dx in near if dy * dx]
        for dy, dx in peers:
            pl.semaphore_signal(barrier, inc=1, device_id=dev(dy, dx), device_id_type=MESH)

    inner = pl.ds(HALO, TILE)
    loads = []
    for c in range(2):
        cols = pl.ds(c * 128, 128)
        loads.append(pltpu.make_async_copy(thick.at[:, cols], nat.at[0, c, inner], l_sem.at[0, c]))
        loads.append(pltpu.make_async_copy(drv.at[:, :, cols], nat.at[pl.ds(1, 2), c, inner], l_sem.at[1, c]))
        loads.append(pltpu.make_async_copy(obs.at[:, :, cols], nat.at[pl.ds(3, 2), c, inner], l_sem.at[2, c]))
    for copy in loads:
        copy.start()

    lane = lax.broadcasted_iota(jnp.int32, (8, 128), 1)
    sub = lax.broadcasted_iota(jnp.int32, (8, 128), 0)
    lane3 = lax.broadcasted_iota(jnp.int32, (LT, 8, 128), 2)

    rates.wait()
    for t in range(32):
        x = c_in[:, pl.ds(t * 128, 128)]
        for k in range(4):
            c_own[k, pl.ds(t, 1)] = x[k:k + 1]
    for k in range(4):
        for g in range(4):
            x = c_own[k, pl.ds(8 * g, 8)]
            right = pltpu.roll(x, 4 * g, 1) if g else x
            left = pltpu.roll(x, 128 - 4 * g, 1) if g else x
            if g == 0:
                side = x
            else:
                side = jnp.where((lane % 64 >= 4 * g) & (lane % 64 < 32), right, side)
                side = jnp.where((lane % 64 >= 32) & (lane % 64 < 64 - 4 * g), left, side)
        c_side[k] = side
        for half in range(2):
            c_ends[k, pl.ds(4 * half, 2)] = c_own[k, pl.ds(30, 2)]
            c_ends[k, pl.ds(4 * half + 2, 2)] = c_own[k, pl.ds(0, 2)]
    eastern = lane % 64 < 32

    seen = [
        [blk[lax.rem(gx + dx + GX, GX), 0, lax.rem(gy + dy, GY)] for dy in range(GY)] for dx in (-1, 0, 1)
    ]

    def tile(dy, dx):
        return seen[dx + 1][dy % GY]

    for off in range(GY):
        pick = {
            (dy, dx): tile(off + dy, dx) & 3 for dy in (-1, 0, 1) for dx in (-1, 0, 1)
        }
        c_send[off, pl.ds(0, 32)] = c_own[pick[0, 0]]
        c_send[off, pl.ds(32, 8)] = jnp.where(eastern, c_side[pick[0, 1]], c_side[pick[0, -1]])
        corner_n = jnp.where(eastern, c_ends[pick[-1, 1]], c_ends[pick[-1, -1]])
        corner_s = jnp.where(eastern, c_ends[pick[1, 1]], c_ends[pick[1, -1]])
        ends = jnp.where(sub < 2, c_ends[pick[-1, 0]], c_ends[pick[1, 0]])
        c_send[off, pl.ds(40, 8)] = jnp.where(sub < 4, ends, jnp.where(sub < 6, corner_n, corner_s))
    gathers = []
    if REMOTE:
        pl.semaphore_wait(barrier, len(peers))
        gathers = [
            remote(c_send.at[off], c_recv.at[off], g_send.at[off], g_recv.at[off], dev(off, 0))
            for off in range(1, GY)
        ]
        for g in gathers:
            g.start()
    c_recv[0] = c_send[0]

    for copy in loads:
        copy.wait()
    shifts = (0, 16, 32, 48, 56)
    for t in range(16):
        w = e = None
        for half in range(2):
            at = pl.ds(HALO + half * 128 + t * 8, 8)
            for f in range(5):
                shift = shifts[f] + 64 * half
                x = nat[f, 0, at]
                y = nat[f, 1, at]
                if shift:
                    x = pltpu.roll(x, shift, 1)
                    y = pltpu.roll(y, 128 - shift, 1)
                w = x if w is None else jnp.where(lane < shift, w, x)
                e = y if e is None else jnp.where(lane >= 128 - shift, e, y)
        pack_w[pl.ds(t * 8, 8), :] = w
        pack_e[pl.ds(t * 8, 8), :] = e

    halos = []
    if REMOTE:
        half = pl.ds(HALO, 128)
        head, tail = pl.ds(0, HALO), pl.ds(112, HALO)
        first, last = pl.ds(0, HALO), pl.ds(TILE + HALO, HALO)
        moves = [
            (pack_e, h_west.at[half], (0, 1)),
            (pack_w, h_east.at[half], (0, -1)),
            (nat.at[:, :, pl.ds(TILE, HALO)], nat.at[:, :, first], (1, 0)),
            (nat.at[:, :, pl.ds(HALO, HALO)], nat.at[:, :, last], (-1, 0)),
            (pack_e.at[tail], h_west.at[first], (1, 1)),
            (pack_e.at[head], h_west.at[last], (-1, 1)),
            (pack_w.at[tail], h_east.at[first], (1, -1)),
            (pack_w.at[head], h_east.at[last], (-1, -1)),
        ]
        halos = [remote(s, d, x_send.at[n], x_recv.at[n], dev(*to)) for n, (s, d, to) in enumerate(moves)]
        for h in halos:
            h.start()

    inside, iced = {}, {}
    for dy, dx in near + [(0, 0)]:
        ok = (gy + dy >= 0) & (gy + dy < GY) & (gx + dx >= 0) & (gx + dx < GX)
        flag = jnp.where(ok, 1.0, 0.0)
        at = ice_ref[jnp.clip(gx + dx, 0, GX - 1), jnp.clip(gy + dy, 0, GY - 1)]
        inside[dy, dx] = flag
        iced[dy, dx] = flag * at.astype(F32)

    def region(cls, table):
        def by_row(dx):
            mid = jnp.full((8, 128), table[0, dx], F32)
            if cls == 0:
                return jnp.where(sub == 0, table[-1, dx], mid)
            if cls == 2:
                return jnp.where(sub == 7, table[1, dx], mid)
            return mid

        center = by_row(0)
        edge = jnp.where(lane < HALO, by_row(1), jnp.where(lane >= 128 - HALO, by_row(-1), 0.0))
        return jnp.stack([center, center, edge])

    for cls in range(3):
        IC[cls] = region(cls, iced)

    def west(x):
        y = pltpu.roll(x, 1, 2)
        return jnp.where(lane3 == 0, jnp.concatenate([y[2:], y[:2]], axis=0), y)

    def east(x):
        y = pltpu.roll(x, 127, 2)
        return jnp.where(lane3 == 127, jnp.concatenate([y[1:], y[:1]], axis=0), y)

    def wrap(refs):
        for ref in refs:
            ref[0] = pltpu.roll(ref[STRIP], 1, 1)
            ref[STRIP + 1] = pltpu.roll(ref[1], 7, 1)

    for h in halos:
        h.wait()

    for ref in (h_west, h_east):
        ref[pl.ds(HALO + 128, 128)] = pltpu.roll(ref[pl.ds(HALO, 128)], 64, 1)
        ref[pl.ds(0, HALO)] = pltpu.roll(ref[pl.ds(0, HALO)], 64, 1)

    keep = [region(cls, inside) for cls in range(3)]
    for i in range(STRIP):
        at = pl.ds(i, 8, stride=STRIP)
        right = h_east[at, :]
        left = h_west[at, :]
        cls = 0 if i < 16 else (1 if i < 20 else 2)
        for f, dst in enumerate((T, FU, FV, OU, OV)):
            r = pltpu.roll(right, 128 - shifts[f], 1) if f else right
            l = pltpu.roll(left, shifts[f], 1) if f else left
            edge = jnp.where(lane < HALO, r, jnp.where(lane >= 128 - HALO, l, 0.0))
            x = jnp.stack([nat[f, 0, at, :], nat[f, 1, at, :], edge])
            if f == 0:
                x = jnp.where(keep[cls] > 0.0, x, 0.0)
            dst[i] = x

    base = float(visc_scale * np.power(strain_floor, -1.0 / 3.0))

    def put(dst, i, u, v):
        U, UE, UW, V, VE, VW = dst
        U[i + 1] = u
        UE[i + 1] = east(u)
        UW[i + 1] = west(u)
        V[i + 1] = v
        VE[i + 1] = east(v)
        VW[i + 1] = west(v)

    def viscosity(src):
        @pl.loop(0, STRIP // MROWS)
        def _(it):
            for k in range(MROWS):
                i = it * MROWS + k
                if src is None:
                    m = (0.5 * base) * T[i]
                else:
                    U, UE, UW, V, VE, VW = src
                    ux = 0.5 * (UE[i + 1] - UW[i + 1])
                    vx = 0.5 * (VE[i + 1] - VW[i + 1])
                    uy = 0.5 * (U[i + 2] - U[i])
                    vy = 0.5 * (V[i + 2] - V[i])
                    sh = uy + vx
                    strain = ux * ux + vy * vy + ux * vy + 0.25 * (sh * sh) + strain_floor
                    m = (0.5 * visc_scale) * T[i] * jnp.exp2(jnp.log2(strain) * (-1.0 / 3.0))
                H[i + 1] = m
                A[i] = east(m)
                B[i] = west(m)

        wrap([H])

    def sweep(src, dst, fu_ref, fv_ref, fresh):
        @pl.loop(0, STRIP // ROWS)
        def _(it):
            b = it * ROWS
            new_u = [[None] * LT for _ in range(ROWS)]
            new_v = [[None] * LT for _ in range(ROWS)]
            n = ROWS + 2
            for c in range(LT):
                h = [H[b + j, c] for j in range(n)]
                face = [h[j] + h[j + 1] for j in range(n - 1)]
                if src is not None:
                    u, ue, uw, v, ve, vw = ([ref[b + j, c] for j in range(n)] for ref in src)
                    q = [h[j] * (ve[j] - vw[j]) for j in range(n)]
                    r = [h[j] * (ue[j] - uw[j]) for j in range(n)]
                for k in range(ROWS):
                    j = k + 1
                    i = b + k
                    a = A[i, c]
                    w_ = B[i, c]
                    fe = h[j] + a
                    fw = h[j] + w_
                    so = face[j]
                    no = face[j - 1]
                    if fresh:
                        ew = fe + fw
                        sn = so + no
                        fr = FR[it * (ROWS // 4) + k // 4, c]
                        step = i // 4
                        cls = jnp.where(step < 4, 0, jnp.where(step < 5, 1, 2))
                        ice = IC[cls, c]
                        if c == 2:
                            fr = jnp.where(ice > 0.0, fr, 1.0)
                        iu = ice / (fr + 4.0 * ew + sn)
                        iv = ice / (fr + ew + 4.0 * sn)
                        IU[i, c] = iu
                        IV[i, c] = iv
                    else:
                        iu = IU[i, c]
                        iv = IV[i, c]
                    fu = fu_ref[i, c]
                    fv = fv_ref[i, c]
                    if src is not None:
                        cu = a * (ve[j + 1] - ve[j - 1]) - w_ * (vw[j + 1] - vw[j - 1]) + 0.5 * (q[j + 1] - q[j - 1])
                        cv = 0.5 * (a * (ue[j + 1] - ue[j - 1]) - w_ * (uw[j + 1] - uw[j - 1])) + (r[j + 1] - r[j - 1])
                        tu = fe * ue[j] + fw * uw[j]
                        su = so * u[j + 1] + no * u[j - 1]
                        tv = fe * ve[j] + fw * vw[j]
                        sv = so * v[j + 1] + no * v[j - 1]
                        fu = fu + 4.0 * tu + su + cu
                        fv = fv + tv + 4.0 * sv + cv
                    new_u[k][c] = iu * fu
                    new_v[k][c] = iv * fv
            for k in range(ROWS):
                put(dst, b + k, jnp.stack(new_u[k]), jnp.stack(new_v[k]))

        wrap(dst)

    zero = (U0, UE0, UW0, V0, VE0, VW0)
    one = (U1, UE1, UW1, V1, VE1, VW1)
    viscosity(None)

    for g in gathers:
        g.wait_recv()

    def heard(dy, dx):
        return lax.rem(gy - tile(dy, dx) // 4 + GY, GY)

    both = jnp.where(eastern, c_recv[heard(0, 1), pl.ds(32, 8)], c_recv[heard(0, -1), pl.ds(32, 8)])
    for g, dx in enumerate((0, 1, -1)):
        row = 0 if dx == 0 else 4
        coarse[g, pl.ds(0, 2)] = c_recv[heard(-1, dx), pl.ds(40, 8)][row:row + 2]
        coarse[g, pl.ds(34, 2)] = c_recv[heard(1, dx), pl.ds(40, 8)][row + 2:row + 4]
        coarse[g, pl.ds(36, 4)] = jnp.zeros((4, 128), F32)
        if dx == 0:
            coarse[g, pl.ds(2, 32)] = c_recv[heard(0, 0), pl.ds(0, 32)]
        else:
            for q in range(4):
                shift = (128 - 4 * q if dx == 1 else 4 * q) % 128
                coarse[g, pl.ds(2 + 8 * q, 8)] = pltpu.roll(both, shift, 1) if shift else both
        flat = jnp.exp(coarse[g])
        cext[g, pl.ds(0, 40, stride=2), :] = flat
        cext[g, pl.ds(1, 40, stride=2), :] = pltpu.roll(flat, 64, 1)
    quarter = lane // 4
    for i in range(GROUP):
        at = pl.ds(i, 8, stride=GROUP)
        mid, right, left = (cext[g, at, :] for g in range(3))
        edges = jnp.where(lane < 64, right, pltpu.roll(left, 64, 1))
        t0 = jnp.take_along_axis(mid, quarter, axis=1)
        t1 = jnp.take_along_axis(mid, quarter + 32, axis=1)
        t2 = jnp.take_along_axis(edges, jnp.where(lane < 64, quarter, 96 + quarter), axis=1)
        FR[i] = jnp.stack([t0, t1, t2])

    sweep(None, one, FU, FV, True)
    sweep(one, zero, FU, FV, False)

    @pl.loop(1, PIC)
    def _(_):
        viscosity(zero)
        sweep(zero, one, FU, FV, True)
        sweep(one, zero, FU, FV, False)

    @pl.loop(0, STRIP // 4)
    def _(it):
        for k in range(4):
            i = it * 4 + k
            u = U0[i + 1]
            v = V0[i + 1]
            FU[i] = u
            FV[i] = v
            at = pl.ds(i, 8, stride=STRIP)
            for c in range(2):
                nat[0, c, at, :] = u[c]
                nat[1, c, at, :] = v[c]
            mu = u - OU[i]
            mv = v - OV[i]
            OU[i] = mu
            OV[i] = mv
            put(one, i, IU[i] * mu, IV[i] * mv)

    stores = []
    for f, dst in enumerate((out_u, out_v)):
        for c in range(2):
            stores.append(
                pltpu.make_async_copy(nat.at[f, c, inner], dst.at[:, pl.ds(c * 128, 128)], o_sem.at[f, c])
            )
    for s in stores:
        s.start()
    wrap(one)

    @pl.loop(0, (ADJ - 2) // 2)
    def _(_):
        sweep(one, zero, OU, OV, False)
        sweep(zero, one, OU, OV, False)

    sweep(one, zero, OU, OV, False)

    for i in range(GROUP):
        total = None
        for k in range(4):
            j = i * 4 + k
            cell = [FU[j, c] * U0[j + 1, c] + FV[j, c] * V0[j + 1, c] for c in range(2)]
            total = cell if total is None else [total[c] + cell[c] for c in range(2)]
        spots = []
        for c in range(2):
            x = -FR[i, c] * total[c]
            x = x + pltpu.roll(x, 127, 1)
            x = x + pltpu.roll(x, 126, 1)
            spots.append(jnp.take_along_axis(x, (lane % 32) * 4, axis=1))
        both = jnp.where(lane % 64 < 32, spots[0], spots[1])
        small[pl.ds(i, 8, stride=GROUP), :] = both
    even = small[pl.ds(4, 32, stride=2), :]
    odd = small[pl.ds(5, 32, stride=2), :]
    wide = lax.broadcasted_iota(jnp.int32, (32, 128), 1)
    grad[...] = jnp.where(wide < 64, even, odd)

    first, second, third = [], [], []
    for g in range(GX):
        part[g] = grad[pl.ds(4 * g, 4), :]
    if REMOTE:
        first = [
            remote(part.at[lax.rem(gx + off, GX)], slots.at[off], b_send.at[off], b_recv.at[off], dev(0, off))
            for off in range(1, GX)
        ]
    for c in first:
        c.start()
    slots[0] = part[gx]
    owners = [blk[lax.rem(gx - off + GX, GX), 0, gy] for off in range(GX)]
    which = lax.broadcasted_iota(jnp.int32, (16, 128), 0) % 4
    for c in first:
        c.wait_recv()
    cells = []
    for t in range(GX):
        x = slots[t]
        cells.append(jnp.concatenate([jnp.broadcast_to(x[j:j + 1], (4, 128)) for j in range(4)], axis=0))
    if REMOTE:
        second = [
            remote(sums.at[off], tiles.at[off], a_send.at[off], a_recv.at[off], dev(off, 0)) for off in range(1, GY)
        ]
    for off in list(range(1, GY)) + [0]:
        lowest = 4 * lax.rem(gy + off, GY)
        total = jnp.zeros((16, 128), F32)
        for t in range(GX):
            total = total + jnp.where(which == owners[t] - lowest, cells[t], 0.0)
        sums[off] = total
        if off > 0 and REMOTE:
            second[off - 1].start()
    total = sums[0]
    for off in range(1, GY):
        if REMOTE:
            second[off - 1].wait_recv()
        total = total + tiles[off]
    red[...] = total
    if REMOTE:
        third = [
            remote(red, gathered.at[gx], d_send.at[off], d_recv.at[off], dev(0, off)) for off in range(1, GX)
        ]
    for c in third:
        c.start()
    gathered[gx] = total
    for c in third:
        c.wait()
    for g in range(GX):
        for j in range(4):
            out_g[:, pl.ds((4 * g + j) * 128, 128)] = gathered[g, pl.ds(4 * j, 4)]
    for c in gathers + first + second:
        c.wait_send()
    for s in stores:
        s.wait()


def call(*operands):
    shape = jax.ShapeDtypeStruct
    dma = pltpu.SemaphoreType.DMA
    hbm = pl.BlockSpec(memory_space=pltpu.HBM)
    smem = pl.BlockSpec(memory_space=pltpu.SMEM)
    vmem = pl.BlockSpec(memory_space=pltpu.VMEM)
    field = pltpu.VMEM((STRIP, LT, 8, 128), F32)
    padded = pltpu.VMEM((STRIP + 2, LT, 8, 128), F32)
    flat = pltpu.VMEM((32, 128), F32)
    return pl.pallas_call(
        kernel,
        name="friction_gradient",
        out_shape=(shape((TILE, TILE), F32), shape((TILE, TILE), F32), shape((4, 4096), F32)),
        in_specs=[smem, smem, hbm, hbm, hbm, hbm],
        out_specs=[hbm, hbm, vmem],
        scratch_shapes=[
            pltpu.VMEM((5, 2, EXT, 128), F32),
            pltpu.VMEM((128, 128), F32),
            pltpu.VMEM((128, 128), F32),
            pltpu.VMEM((EXT, 128), F32),
            pltpu.VMEM((EXT, 128), F32),
            pltpu.VMEM((4, 4096), F32),
            pltpu.VMEM((4, 32, 128), F32),
            pltpu.VMEM((4, 8, 128), F32),
            pltpu.VMEM((4, 8, 128), F32),
            pltpu.VMEM((GY, 48, 128), F32),
            pltpu.VMEM((GY, 48, 128), F32),
            pltpu.VMEM((3, 40, 128), F32),
            pltpu.VMEM((3, 80, 128), F32),
            field, field, field, field, field,
            pltpu.VMEM((GROUP, LT, 8, 128), F32),
            pltpu.VMEM((3, LT, 8, 128), F32),
            padded, field, field, field, field,
        ] + [padded] * 12 + [
            pltpu.VMEM((72, 128), F32),
            flat,
            pltpu.VMEM((GY, 16, 128), F32),
            pltpu.VMEM((GY, 16, 128), F32),
            pltpu.VMEM((GX, 4, 128), F32),
            pltpu.VMEM((GX, 4, 128), F32),
            pltpu.VMEM((16, 128), F32),
            pltpu.VMEM((GX, 16, 128), F32),
            dma, dma((3, 2)), dma((2, 2)),
            dma((GY,)), dma((GY,)), dma((8,)), dma((8,)),
            dma((GY,)), dma((GY,)), dma((GX,)), dma((GX,)), dma((GX,)), dma((GX,)),
        ],
        compiler_params=pltpu.CompilerParams(
            vmem_limit_bytes=60 << 20,
            **(dict(collective_id=0, has_side_effects=True) if REMOTE else {}),
        ),
    )(*operands)


def per_device(thickness, driving, observed, control, ice_mask, tile_block):
    return call(
        tile_block.transpose(1, 2, 0), ice_mask.T, thickness, driving, observed, control
    )


def solution(mesh):
    return jax.shard_map(
        per_device,
        mesh=mesh,
        in_specs=(P("gy", "gx"), P(None, "gy", "gx"), P(None, "gy", "gx"), P("gy", None), P(), P()),
        out_specs=(P("gy", "gx"), P("gy", "gx"), P("gy", None)),
        check_vma=False,
    )
```

```python
import jax
import jax.numpy as jnp
import numpy as np
from jax import lax
from jax.experimental import pallas as pl
from jax.experimental.pallas import tpu as pltpu
from jax.sharding import PartitionSpec as P

TILE = 256
HALO = 16
EXT = TILE + 2 * HALO
STRIP = EXT // 8
GROUP = STRIP // 4
PIC = 4
ADJ = 6
GX = 8
GY = 16
ROWS = 3
REMOTE = True
MESH = pl.DeviceIdType.MESH
F32 = jnp.float32

visc_scale = 0.1
strain_floor = 0.05


def kernel(
    blk, ice_ref, thick, drv, obs, ctl,
    out_u, out_v, out_g,
    nat, pack_w, pack_e, h_west, h_east, c_in, c_own, c_side, c_ends, c_send, c_recv, coarse, cext,
    T, FU, FV, OU, OV, FR, IC, H, A, B, IU, IV,
    U0, UE0, UW0, V0, VE0, VW0, U1, UE1, UW1, V1, VE1, VW1,
    small, grad, sums, tiles, part, slots, red, gathered,
    k_sem, l_sem, o_sem, g_send, g_recv, x_send, x_recv,
    a_send, a_recv, b_send, b_recv, d_send, d_recv,
):
    gx = lax.axis_index("gx")
    gy = lax.axis_index("gy")

    def dev(dy, dx):
        return (lax.rem(gx + dx + GX, GX), lax.rem(gy + dy + GY, GY))

    def remote(src, dst, ss, rs, to):
        return pltpu.make_async_remote_copy(
            src_ref=src, dst_ref=dst, send_sem=ss, recv_sem=rs, device_id=to, device_id_type=MESH
        )

    rates = pltpu.make_async_copy(ctl, c_in, k_sem)
    rates.start()
    near = [(dy, dx) for dy in (-1, 0, 1) for dx in (-1, 0, 1) if (dy, dx) != (0, 0)]
    if REMOTE:
        barrier = pltpu.get_barrier_semaphore()
        peers = [(dy, 0) for dy in range(1, GY)] + [(0, dx) for dx in range(1, GX)]
        peers += [(dy, dx) for dy, dx in near if dy * dx]
        for dy, dx in peers:
            pl.semaphore_signal(barrier, inc=1, device_id=dev(dy, dx), device_id_type=MESH)

    inner = pl.ds(HALO, TILE)
    loads = []
    for c in range(2):
        cols = pl.ds(c * 128, 128)
        loads.append(pltpu.make_async_copy(thick.at[:, cols], nat.at[0, c, inner], l_sem.at[0, c]))
        loads.append(pltpu.make_async_copy(drv.at[:, :, cols], nat.at[pl.ds(1, 2), c, inner], l_sem.at[1, c]))
        loads.append(pltpu.make_async_copy(obs.at[:, :, cols], nat.at[pl.ds(3, 2), c, inner], l_sem.at[2, c]))
    for copy in loads:
        copy.start()

    lane = lax.broadcasted_iota(jnp.int32, (8, 128), 1)
    sub = lax.broadcasted_iota(jnp.int32, (8, 128), 0)

    rates.wait()
    for t in range(32):
        x = c_in[:, pl.ds(t * 128, 128)]
        for k in range(4):
            c_own[k, pl.ds(t, 1)] = x[k:k + 1]
    for k in range(4):
        for g in range(4):
            x = c_own[k, pl.ds(8 * g, 8)]
            right = pltpu.roll(x, 4 * g, 1) if g else x
            left = pltpu.roll(x, 128 - 4 * g, 1) if g else x
            if g == 0:
                side = x
            else:
                side = jnp.where((lane % 64 >= 4 * g) & (lane % 64 < 32), right, side)
                side = jnp.where((lane % 64 >= 32) & (lane % 64 < 64 - 4 * g), left, side)
        c_side[k] = side
        for half in range(2):
            c_ends[k, pl.ds(4 * half, 2)] = c_own[k, pl.ds(30, 2)]
            c_ends[k, pl.ds(4 * half + 2, 2)] = c_own[k, pl.ds(0, 2)]
    eastern = lane % 64 < 32

    seen = [
        [blk[lax.rem(gx + dx + GX, GX), 0, lax.rem(gy + dy, GY)] for dy in range(GY)] for dx in (-1, 0, 1)
    ]

    def tile(dy, dx):
        return seen[dx + 1][dy % GY]

    for off in range(GY):
        pick = {
            (dy, dx): tile(off + dy, dx) & 3 for dy in (-1, 0, 1) for dx in (-1, 0, 1)
        }
        c_send[off, pl.ds(0, 32)] = c_own[pick[0, 0]]
        c_send[off, pl.ds(32, 8)] = jnp.where(eastern, c_side[pick[0, 1]], c_side[pick[0, -1]])
        corner_n = jnp.where(eastern, c_ends[pick[-1, 1]], c_ends[pick[-1, -1]])
        corner_s = jnp.where(eastern, c_ends[pick[1, 1]], c_ends[pick[1, -1]])
        ends = jnp.where(sub < 2, c_ends[pick[-1, 0]], c_ends[pick[1, 0]])
        c_send[off, pl.ds(40, 8)] = jnp.where(sub < 4, ends, jnp.where(sub < 6, corner_n, corner_s))
    gathers = []
    if REMOTE:
        pl.semaphore_wait(barrier, len(peers))
        gathers = [
            remote(c_send.at[off], c_recv.at[off], g_send.at[off], g_recv.at[off], dev(off, 0))
            for off in range(1, GY)
        ]
        for g in gathers:
            g.start()
    c_recv[0] = c_send[0]

    for copy in loads:
        copy.wait()
    shifts = (0, 16, 32, 48, 56)
    for t in range(16):
        w = e = None
        for half in range(2):
            at = pl.ds(HALO + half * 128 + t * 8, 8)
            for f in range(5):
                shift = shifts[f] + 64 * half
                x = nat[f, 0, at]
                y = nat[f, 1, at]
                if shift:
                    x = pltpu.roll(x, shift, 1)
                    y = pltpu.roll(y, 128 - shift, 1)
                w = x if w is None else jnp.where(lane < shift, w, x)
                e = y if e is None else jnp.where(lane >= 128 - shift, e, y)
        pack_w[pl.ds(t * 8, 8), :] = w
        pack_e[pl.ds(t * 8, 8), :] = e

    halos = []
    if REMOTE:
        half = pl.ds(HALO, 128)
        head, tail = pl.ds(0, HALO), pl.ds(112, HALO)
        first, last = pl.ds(0, HALO), pl.ds(TILE + HALO, HALO)
        moves = [
            (pack_e, h_west.at[half], (0, 1)),
            (pack_w, h_east.at[half], (0, -1)),
            (nat.at[:, :, pl.ds(TILE, HALO)], nat.at[:, :, first], (1, 0)),
            (nat.at[:, :, pl.ds(HALO, HALO)], nat.at[:, :, last], (-1, 0)),
            (pack_e.at[tail], h_west.at[first], (1, 1)),
            (pack_e.at[head], h_west.at[last], (-1, 1)),
            (pack_w.at[tail], h_east.at[first], (1, -1)),
            (pack_w.at[head], h_east.at[last], (-1, -1)),
        ]
        halos = [remote(s, d, x_send.at[n], x_recv.at[n], dev(*to)) for n, (s, d, to) in enumerate(moves)]
        for h in halos:
            h.start()

    inside, iced = {}, {}
    for dy, dx in near + [(0, 0)]:
        ok = (gy + dy >= 0) & (gy + dy < GY) & (gx + dx >= 0) & (gx + dx < GX)
        flag = jnp.where(ok, 1.0, 0.0)
        at = ice_ref[jnp.clip(gx + dx, 0, GX - 1), jnp.clip(gy + dy, 0, GY - 1)]
        inside[dy, dx] = flag
        iced[dy, dx] = flag * at.astype(F32)

    def m(i, c):
        return 2 * (i + 1) + c

    def p(i):
        return 2 * (STRIP + 2) + 1 + i

    within = lane % 32
    block = lane // 32

    def region(i, table):
        base = jnp.full((8, 128), table[0, 0], F32)
        if i < HALO:
            return jnp.where(sub == 0, table[-1, 0], base)
        if i >= TILE + HALO - 7 * STRIP:
            return jnp.where(sub == 7, table[1, 0], base)
        return base

    def side_region(i, table):
        row = sub * STRIP + block * GROUP + i

        def by_row(dx):
            return jnp.where(
                row < HALO, table[-1, dx], jnp.where(row < HALO + TILE, table[0, dx], table[1, dx])
            )

        return jnp.where(within < HALO, by_row(1), by_row(-1))

    def shifts_of(t0, t1, x):
        w0 = [pltpu.roll(t, 1, 1) for t in t0]
        w1 = [pltpu.roll(t, 1, 1) for t in t1]
        e0 = [pltpu.roll(t, 127, 1) for t in t0]
        e1 = [pltpu.roll(t, 127, 1) for t in t1]
        wx = pltpu.roll(x, 1, 1)
        ex = pltpu.roll(x, 127, 1)
        west = [[], []]
        east = [[], []]
        west_x, east_x = wx, ex
        for g in range(4):
            from_x = wx if g == 3 else pltpu.roll(x, 97 - 32 * g, 1)
            west[0].append(jnp.where(lane == 0, from_x, w0[g]))
            west[1].append(jnp.where(lane == 0, w0[g], w1[g]))
            edge = w1[g] if g == 0 else pltpu.roll(t1[g], 32 * g + 1, 1)
            west_x = jnp.where(lane == 32 * g, edge, west_x)
            from_x = ex if g == 0 else pltpu.roll(x, 127 - 32 * g, 1)
            east[0].append(jnp.where(lane == 127, e1[g], e0[g]))
            east[1].append(jnp.where(lane == 127, from_x, e1[g]))
            edge = e0[g] if g == 3 else pltpu.roll(t0[g], 32 * g + 31, 1)
            east_x = jnp.where(lane == 32 * g + 31, edge, east_x)
        return east, east_x, west, west_x

    def keep_all(ref, i, t, x):
        for g in range(4):
            for c in range(2):
                ref[m(GROUP * g + i, c)] = t[c][g]
        ref[p(i)] = x

    def put(dst, i, u, ux, v, vx):
        for refs, t, x in ((dst[:3], u, ux), (dst[3:], v, vx)):
            east, east_x, west, west_x = shifts_of(t[0], t[1], x)
            keep_all(refs[0], i, t, x)
            keep_all(refs[1], i, east, east_x)
            keep_all(refs[2], i, west, west_x)

    def wrap(refs):
        for ref in refs:
            for c in range(2):
                ref[m(-1, c)] = pltpu.roll(ref[m(STRIP - 1, c)], 1, 0)
                ref[m(STRIP, c)] = pltpu.roll(ref[m(0, c)], 7, 0)
            y = pltpu.roll(ref[p(GROUP - 1)], 32, 1)
            ref[p(-1)] = jnp.where(lane < 32, pltpu.roll(y, 1, 0), y)
            y = pltpu.roll(ref[p(0)], 96, 1)
            ref[p(GROUP)] = jnp.where(lane >= 96, pltpu.roll(y, 7, 0), y)

    for h in halos:
        h.wait()

    for ref in (h_west, h_east):
        ref[pl.ds(HALO + 128, 128)] = pltpu.roll(ref[pl.ds(HALO, 128)], 64, 1)
        ref[pl.ds(0, HALO)] = pltpu.roll(ref[pl.ds(0, HALO)], 64, 1)

    fields = (T, FU, FV, OU, OV)
    for i in range(STRIP):
        at = pl.ds(i, 8, stride=STRIP)
        for c in range(2):
            for f, dst in enumerate(fields):
                dst[m(i, c)] = nat[f, c, at, :]
    for i in range(GROUP):
        right = [h_east[pl.ds(GROUP * g + i, 8, stride=STRIP), :] for g in range(4)]
        left = [h_west[pl.ds(GROUP * g + i, 8, stride=STRIP), :] for g in range(4)]
        for f, dst in enumerate(fields):
            x = None
            for g in range(4):
                r = (32 * g - shifts[f]) % 128
                l = (32 * g + HALO - 112 + shifts[f]) % 128
                r = pltpu.roll(right[g], r, 1) if r else right[g]
                l = pltpu.roll(left[g], l, 1) if l else left[g]
                y = jnp.where(within < HALO, r, l)
                x = y if x is None else jnp.where(block == g, y, x)
            if f == 0:
                x = jnp.where(side_region(i, inside) > 0.0, x, 0.0)
            dst[p(i)] = x
    for i in list(range(HALO)) + list(range(TILE + HALO - 7 * STRIP, STRIP)):
        keep = region(i, inside) > 0.0
        for c in range(2):
            T[m(i, c)] = jnp.where(keep, T[m(i, c)], 0.0)

    base = float(visc_scale * np.power(strain_floor, -1.0 / 3.0))
    every = [[m(GROUP * g + i, c) for c in range(2) for g in range(4)] + [p(i)] for i in range(GROUP)]

    def step_of(at, by):
        return at + 2 * by if at < p(-1) else at + by

    def split(values):
        return [values[:4], values[4:8]], values[8]

    def viscosity(src):
        for spot, i in enumerate([0, GROUP - 1] + list(range(1, GROUP - 1))):
            values = []
            for at in every[i]:
                if src is None:
                    values.append((0.5 * base) * T[at])
                    continue
                U, UE, UW, V, VE, VW = src
                ux = 0.5 * (UE[at] - UW[at])
                vx = 0.5 * (VE[at] - VW[at])
                uy = 0.5 * (U[step_of(at, 1)] - U[step_of(at, -1)])
                vy = 0.5 * (V[step_of(at, 1)] - V[step_of(at, -1)])
                sh = uy + vx
                strain = ux * ux + vy * vy + ux * vy + 0.25 * (sh * sh) + strain_floor
                values.append((0.5 * visc_scale) * T[at] * jnp.exp2(jnp.log2(strain) * (-1.0 / 3.0)))
            t, x = split(values)
            east, east_x, west, west_x = shifts_of(t[0], t[1], x)
            keep_all(H, i, t, x)
            keep_all(A, i, east, east_x)
            keep_all(B, i, west, west_x)
            if spot == 1:
                wrap([H])

    def sweep(src, dst, fu_ref, fv_ref, fresh):
        starts = list(range(0, GROUP, ROWS))
        for spot, s in enumerate([starts[0], starts[-1]] + starts[1:-1]):
            new_u = [[None] * 9 for _ in range(ROWS)]
            new_v = [[None] * 9 for _ in range(ROWS)]
            n = ROWS + 2
            for lot in range(9):
                spots = [step_of(every[s][lot], j - 1) for j in range(n)]
                h = [H[at] for at in spots]
                face = [h[j] + h[j + 1] for j in range(n - 1)]
                if src is not None:
                    u, ue, uw, v, ve, vw = ([ref[at] for at in spots] for ref in src)
                    q = [h[j] * (ve[j] - vw[j]) for j in range(n)]
                    r = [h[j] * (ue[j] - uw[j]) for j in range(n)]
                for k in range(ROWS):
                    j = k + 1
                    at = spots[j]
                    a = A[at]
                    w_ = B[at]
                    fe = h[j] + a
                    fw = h[j] + w_
                    so = face[j]
                    no = face[j - 1]
                    if fresh:
                        ew = fe + fw
                        sn = so + no
                        step = s + k
                        if lot < 8:
                            step = GROUP * (lot % 4) + step
                            fr = FR[2 * (step // 4) + lot // 4]
                            ice = region(step, iced)
                        else:
                            fr = FR[2 * GROUP + step]
                            ice = IC[step]
                        iu = ice / (fr + 4.0 * ew + sn)
                        iv = ice / (fr + ew + 4.0 * sn)
                        IU[at] = iu
                        IV[at] = iv
                    else:
                        iu = IU[at]
                        iv = IV[at]
                    fu = fu_ref[at]
                    fv = fv_ref[at]
                    if src is not None:
                        cu = a * (ve[j + 1] - ve[j - 1]) - w_ * (vw[j + 1] - vw[j - 1]) + 0.5 * (q[j + 1] - q[j - 1])
                        cv = 0.5 * (a * (ue[j + 1] - ue[j - 1]) - w_ * (uw[j + 1] - uw[j - 1])) + (r[j + 1] - r[j - 1])
                        tu = fe * ue[j] + fw * uw[j]
                        su = so * u[j + 1] + no * u[j - 1]
                        tv = fe * ve[j] + fw * vw[j]
                        sv = so * v[j + 1] + no * v[j - 1]
                        fu = fu + 4.0 * tu + su + cu
                        fv = fv + tv + 4.0 * sv + cv
                    new_u[k][lot] = iu * fu
                    new_v[k][lot] = iv * fv
            for k in range(ROWS):
                put(dst, s + k, *split(new_u[k]), *split(new_v[k]))
            if spot == 1:
                wrap(dst)

    zero = (U0, UE0, UW0, V0, VE0, VW0)
    one = (U1, UE1, UW1, V1, VE1, VW1)
    viscosity(None)

    for g in gathers:
        g.wait_recv()

    def heard(dy, dx):
        return lax.rem(gy - tile(dy, dx) // 4 + GY, GY)

    both = jnp.where(eastern, c_recv[heard(0, 1), pl.ds(32, 8)], c_recv[heard(0, -1), pl.ds(32, 8)])
    for g, dx in enumerate((0, 1, -1)):
        row = 0 if dx == 0 else 4
        coarse[g, pl.ds(0, 2)] = c_recv[heard(-1, dx), pl.ds(40, 8)][row:row + 2]
        coarse[g, pl.ds(34, 2)] = c_recv[heard(1, dx), pl.ds(40, 8)][row + 2:row + 4]
        coarse[g, pl.ds(36, 4)] = jnp.zeros((4, 128), F32)
        if dx == 0:
            coarse[g, pl.ds(2, 32)] = c_recv[heard(0, 0), pl.ds(0, 32)]
        else:
            for q in range(4):
                shift = (128 - 4 * q if dx == 1 else 4 * q) % 128
                coarse[g, pl.ds(2 + 8 * q, 8)] = pltpu.roll(both, shift, 1) if shift else both
        flat = jnp.exp(coarse[g])
        cext[g, pl.ds(0, 40, stride=2), :] = flat
        cext[g, pl.ds(1, 40, stride=2), :] = pltpu.roll(flat, 64, 1)
    quarter = lane // 4
    sides = []
    for i in range(GROUP):
        at = pl.ds(i, 8, stride=GROUP)
        mid, right, left = (cext[g, at, :] for g in range(3))
        edges = jnp.where(lane < 64, right, pltpu.roll(left, 64, 1))
        FR[2 * i] = jnp.take_along_axis(mid, quarter, axis=1)
        FR[2 * i + 1] = jnp.take_along_axis(mid, quarter + 32, axis=1)
        sides.append(
            jnp.take_along_axis(edges, jnp.where(within < HALO, within // 4, 120 + within // 4), axis=1)
        )
    for i in range(GROUP):
        x = sides[i // 4]
        for g in range(1, 4):
            x = jnp.where(block == g, sides[(GROUP * g + i) // 4], x)
        FR[2 * GROUP + i] = x
        IC[i] = side_region(i, iced)

    sweep(None, one, FU, FV, True)
    sweep(one, zero, FU, FV, False)

    @pl.loop(1, PIC)
    def _(_):
        viscosity(zero)
        sweep(zero, one, FU, FV, True)
        sweep(one, zero, FU, FV, False)

    for i in range(GROUP):
        new_u, new_v = [], []
        for at in every[i]:
            u = U0[at]
            v = V0[at]
            FU[at] = u
            FV[at] = v
            mu = u - OU[at]
            mv = v - OV[at]
            OU[at] = mu
            OV[at] = mv
            new_u.append(IU[at] * mu)
            new_v.append(IV[at] * mv)
        put(one, i, *split(new_u), *split(new_v))
    for i in range(STRIP):
        at = pl.ds(i, 8, stride=STRIP)
        for c in range(2):
            nat[0, c, at, :] = FU[m(i, c)]
            nat[1, c, at, :] = FV[m(i, c)]

    stores = []
    for f, dst in enumerate((out_u, out_v)):
        for c in range(2):
            stores.append(
                pltpu.make_async_copy(nat.at[f, c, inner], dst.at[:, pl.ds(c * 128, 128)], o_sem.at[f, c])
            )
    for s in stores:
        s.start()
    wrap(one)

    @pl.loop(0, (ADJ - 2) // 2)
    def _(_):
        sweep(one, zero, OU, OV, False)
        sweep(zero, one, OU, OV, False)

    sweep(one, zero, OU, OV, False)

    for i in range(GROUP):
        total = None
        for k in range(4):
            j = i * 4 + k
            cell = [FU[m(j, c)] * U0[m(j, c)] + FV[m(j, c)] * V0[m(j, c)] for c in range(2)]
            total = cell if total is None else [total[c] + cell[c] for c in range(2)]
        spots = []
        for c in range(2):
            x = -FR[2 * i + c] * total[c]
            x = x + pltpu.roll(x, 127, 1)
            x = x + pltpu.roll(x, 126, 1)
            spots.append(jnp.take_along_axis(x, (lane % 32) * 4, axis=1))
        both = jnp.where(lane % 64 < 32, spots[0], spots[1])
        small[pl.ds(i, 8, stride=GROUP), :] = both
    even = small[pl.ds(4, 32, stride=2), :]
    odd = small[pl.ds(5, 32, stride=2), :]
    wide = lax.broadcasted_iota(jnp.int32, (32, 128), 1)
    grad[...] = jnp.where(wide < 64, even, odd)

    first, second, third = [], [], []
    for g in range(GX):
        part[g] = grad[pl.ds(4 * g, 4), :]
    if REMOTE:
        first = [
            remote(part.at[lax.rem(gx + off, GX)], slots.at[off], b_send.at[off], b_recv.at[off], dev(0, off))
            for off in range(1, GX)
        ]
    for c in first:
        c.start()
    slots[0] = part[gx]
    owners = [blk[lax.rem(gx - off + GX, GX), 0, gy] for off in range(GX)]
    which = lax.broadcasted_iota(jnp.int32, (16, 128), 0) % 4
    for c in first:
        c.wait_recv()
    cells = []
    for t in range(GX):
        x = slots[t]
        cells.append(jnp.concatenate([jnp.broadcast_to(x[j:j + 1], (4, 128)) for j in range(4)], axis=0))
    if REMOTE:
        second = [
            remote(sums.at[off], tiles.at[off], a_send.at[off], a_recv.at[off], dev(off, 0)) for off in range(1, GY)
        ]
    for off in list(range(1, GY)) + [0]:
        lowest = 4 * lax.rem(gy + off, GY)
        total = jnp.zeros((16, 128), F32)
        for t in range(GX):
            total = total + jnp.where(which == owners[t] - lowest, cells[t], 0.0)
        sums[off] = total
        if off > 0 and REMOTE:
            second[off - 1].start()
    total = sums[0]
    for off in range(1, GY):
        if REMOTE:
            second[off - 1].wait_recv()
        total = total + tiles[off]
    red[...] = total
    if REMOTE:
        third = [
            remote(red, gathered.at[gx], d_send.at[off], d_recv.at[off], dev(0, off)) for off in range(1, GX)
        ]
    for c in third:
        c.start()
    gathered[gx] = total
    for c in third:
        c.wait()
    for g in range(GX):
        for j in range(4):
            out_g[:, pl.ds((4 * g + j) * 128, 128)] = gathered[g, pl.ds(4 * j, 4)]
    for c in gathers + first + second:
        c.wait_send()
    for s in stores:
        s.wait()


def call(*operands):
    shape = jax.ShapeDtypeStruct
    dma = pltpu.SemaphoreType.DMA
    hbm = pl.BlockSpec(memory_space=pltpu.HBM)
    smem = pl.BlockSpec(memory_space=pltpu.SMEM)
    vmem = pl.BlockSpec(memory_space=pltpu.VMEM)
    field = pltpu.VMEM((2 * (STRIP + 2) + GROUP + 2, 8, 128), F32)
    flat = pltpu.VMEM((32, 128), F32)
    return pl.pallas_call(
        kernel,
        name="friction_gradient",
        out_shape=(shape((TILE, TILE), F32), shape((TILE, TILE), F32), shape((4, 4096), F32)),
        in_specs=[smem, smem, hbm, hbm, hbm, hbm],
        out_specs=[hbm, hbm, vmem],
        scratch_shapes=[
            pltpu.VMEM((5, 2, EXT, 128), F32),
            pltpu.VMEM((128, 128), F32),
            pltpu.VMEM((128, 128), F32),
            pltpu.VMEM((EXT, 128), F32),
            pltpu.VMEM((EXT, 128), F32),
            pltpu.VMEM((4, 4096), F32),
            pltpu.VMEM((4, 32, 128), F32),
            pltpu.VMEM((4, 8, 128), F32),
            pltpu.VMEM((4, 8, 128), F32),
            pltpu.VMEM((GY, 48, 128), F32),
            pltpu.VMEM((GY, 48, 128), F32),
            pltpu.VMEM((3, 40, 128), F32),
            pltpu.VMEM((3, 80, 128), F32),
            field, field, field, field, field,
            pltpu.VMEM((3 * GROUP, 8, 128), F32),
            pltpu.VMEM((GROUP, 8, 128), F32),
            field, field, field, field, field,
        ] + [field] * 12 + [
            pltpu.VMEM((72, 128), F32),
            flat,
            pltpu.VMEM((GY, 16, 128), F32),
            pltpu.VMEM((GY, 16, 128), F32),
            pltpu.VMEM((GX, 4, 128), F32),
            pltpu.VMEM((GX, 4, 128), F32),
            pltpu.VMEM((16, 128), F32),
            pltpu.VMEM((GX, 16, 128), F32),
            dma, dma((3, 2)), dma((2, 2)),
            dma((GY,)), dma((GY,)), dma((8,)), dma((8,)),
            dma((GY,)), dma((GY,)), dma((GX,)), dma((GX,)), dma((GX,)), dma((GX,)),
        ],
        compiler_params=pltpu.CompilerParams(
            vmem_limit_bytes=60 << 20,
            **(dict(collective_id=0, has_side_effects=True) if REMOTE else {}),
        ),
    )(*operands)


def per_device(thickness, driving, observed, control, ice_mask, tile_block):
    return call(
        tile_block.transpose(1, 2, 0), ice_mask.T, thickness, driving, observed, control
    )


def solution(mesh):
    return jax.shard_map(
        per_device,
        mesh=mesh,
        in_specs=(P("gy", "gx"), P(None, "gy", "gx"), P(None, "gy", "gx"), P("gy", None), P(), P()),
        out_specs=(P("gy", "gx"), P("gy", "gx"), P("gy", None)),
        check_vma=False,
    )
```

```python
import jax
import jax.numpy as jnp
import numpy as np
from jax import lax
from jax.experimental import pallas as pl
from jax.experimental.pallas import tpu as pltpu
from jax.sharding import PartitionSpec as P

TILE = 256
HALO = 16
EXT = TILE + 2 * HALO
STRIP = EXT // 8
GROUP = STRIP // 4
PIC = 4
ADJ = 6
GX = 8
GY = 16
ROWS = 3
REMOTE = True
MESH = pl.DeviceIdType.MESH
F32 = jnp.float32

visc_scale = 0.1
strain_floor = 0.05


def kernel(
    blk, ice_ref, thick, drv, obs, ctl,
    out_u, out_v, out_g,
    nat, pack_w, pack_e, h_west, h_east, c_in, c_own, c_side, c_ends, c_send, c_recv, coarse, cext,
    T, FU, FV, OU, OV, FR, IC, H, A, B, IU, IV,
    U0, UE0, UW0, V0, VE0, VW0, U1, UE1, UW1, V1, VE1, VW1,
    small, grad, sums, tiles, part, slots, red, gathered,
    k_sem, l_sem, o_sem, g_send, g_recv, x_send, x_recv,
    a_send, a_recv, b_send, b_recv, d_send, d_recv,
):
    gx = lax.axis_index("gx")
    gy = lax.axis_index("gy")

    def dev(dy, dx):
        return (lax.rem(gx + dx + GX, GX), lax.rem(gy + dy + GY, GY))

    def remote(src, dst, ss, rs, to):
        return pltpu.make_async_remote_copy(
            src_ref=src, dst_ref=dst, send_sem=ss, recv_sem=rs, device_id=to, device_id_type=MESH
        )

    rates = pltpu.make_async_copy(ctl, c_in, k_sem)
    rates.start()
    near = [(dy, dx) for dy in (-1, 0, 1) for dx in (-1, 0, 1) if (dy, dx) != (0, 0)]
    if REMOTE:
        barrier = pltpu.get_barrier_semaphore()
        peers = [(dy, 0) for dy in range(1, GY)] + [(0, dx) for dx in range(1, GX)]
        peers += [(dy, dx) for dy, dx in near if dy * dx]
        for dy, dx in peers:
            pl.semaphore_signal(barrier, inc=1, device_id=dev(dy, dx), device_id_type=MESH)

    inner = pl.ds(HALO, TILE)
    loads = []
    for c in range(2):
        cols = pl.ds(c * 128, 128)
        loads.append(pltpu.make_async_copy(thick.at[:, cols], nat.at[0, c, inner], l_sem.at[0, c]))
        loads.append(pltpu.make_async_copy(drv.at[:, :, cols], nat.at[pl.ds(1, 2), c, inner], l_sem.at[1, c]))
        loads.append(pltpu.make_async_copy(obs.at[:, :, cols], nat.at[pl.ds(3, 2), c, inner], l_sem.at[2, c]))
    for copy in loads:
        copy.start()

    lane = lax.broadcasted_iota(jnp.int32, (8, 128), 1)
    sub = lax.broadcasted_iota(jnp.int32, (8, 128), 0)

    rates.wait()
    for t in range(32):
        x = c_in[:, pl.ds(t * 128, 128)]
        for k in range(4):
            c_own[k, pl.ds(t, 1)] = x[k:k + 1]
    for k in range(4):
        for g in range(4):
            x = c_own[k, pl.ds(8 * g, 8)]
            right = pltpu.roll(x, 4 * g, 1) if g else x
            left = pltpu.roll(x, 128 - 4 * g, 1) if g else x
            if g == 0:
                side = x
            else:
                side = jnp.where((lane % 64 >= 4 * g) & (lane % 64 < 32), right, side)
                side = jnp.where((lane % 64 >= 32) & (lane % 64 < 64 - 4 * g), left, side)
        c_side[k] = side
        for half in range(2):
            c_ends[k, pl.ds(4 * half, 2)] = c_own[k, pl.ds(30, 2)]
            c_ends[k, pl.ds(4 * half + 2, 2)] = c_own[k, pl.ds(0, 2)]
    eastern = lane % 64 < 32

    seen = [
        [blk[lax.rem(gx + dx + GX, GX), 0, lax.rem(gy + dy, GY)] for dy in range(GY)] for dx in (-1, 0, 1)
    ]

    def tile(dy, dx):
        return seen[dx + 1][dy % GY]

    gathers = []
    if REMOTE:
        pl.semaphore_wait(barrier, len(peers))
        gathers = [
            remote(c_send.at[off], c_recv.at[off], g_send.at[off], g_recv.at[off], dev(off, 0))
            for off in range(1, GY)
        ]
    for off in list(range(1, GY)) + [0]:
        pick = {
            (dy, dx): tile(off + dy, dx) & 3 for dy in (-1, 0, 1) for dx in (-1, 0, 1)
        }
        c_send[off, pl.ds(0, 32)] = c_own[pick[0, 0]]
        c_send[off, pl.ds(32, 8)] = jnp.where(eastern, c_side[pick[0, 1]], c_side[pick[0, -1]])
        corner_n = jnp.where(eastern, c_ends[pick[-1, 1]], c_ends[pick[-1, -1]])
        corner_s = jnp.where(eastern, c_ends[pick[1, 1]], c_ends[pick[1, -1]])
        ends = jnp.where(sub < 2, c_ends[pick[-1, 0]], c_ends[pick[1, 0]])
        c_send[off, pl.ds(40, 8)] = jnp.where(sub < 4, ends, jnp.where(sub < 6, corner_n, corner_s))
        if off > 0 and REMOTE:
            gathers[off - 1].start()
    c_recv[0] = c_send[0]

    for copy in loads:
        copy.wait()

    def send(at, moves):
        copies = [
            remote(s, d, x_send.at[at + n], x_recv.at[at + n], dev(*to)) for n, (s, d, to) in enumerate(moves)
        ]
        for c in copies:
            c.start()
        return copies

    halos = []
    first, last = pl.ds(0, HALO), pl.ds(TILE + HALO, HALO)
    if REMOTE:
        halos += send(0, [
            (nat.at[:, :, pl.ds(TILE, HALO)], nat.at[:, :, first], (1, 0)),
            (nat.at[:, :, pl.ds(HALO, HALO)], nat.at[:, :, last], (-1, 0)),
        ])
    shifts = (0, 16, 32, 48, 56)
    for t in range(16):
        w = e = None
        for half in range(2):
            at = pl.ds(HALO + half * 128 + t * 8, 8)
            for f in range(5):
                shift = shifts[f] + 64 * half
                x = nat[f, 0, at]
                y = nat[f, 1, at]
                if shift:
                    x = pltpu.roll(x, shift, 1)
                    y = pltpu.roll(y, 128 - shift, 1)
                w = x if w is None else jnp.where(lane < shift, w, x)
                e = y if e is None else jnp.where(lane >= 128 - shift, e, y)
        pack_w[pl.ds(t * 8, 8), :] = w
        pack_e[pl.ds(t * 8, 8), :] = e

    if REMOTE:
        half = pl.ds(HALO, 128)
        head, tail = pl.ds(0, HALO), pl.ds(112, HALO)
        halos += send(2, [
            (pack_e, h_west.at[half], (0, 1)),
            (pack_w, h_east.at[half], (0, -1)),
            (pack_e.at[tail], h_west.at[first], (1, 1)),
            (pack_e.at[head], h_west.at[last], (-1, 1)),
            (pack_w.at[tail], h_east.at[first], (1, -1)),
            (pack_w.at[head], h_east.at[last], (-1, -1)),
        ])

    inside, iced = {}, {}
    for dy, dx in near + [(0, 0)]:
        ok = (gy + dy >= 0) & (gy + dy < GY) & (gx + dx >= 0) & (gx + dx < GX)
        flag = jnp.where(ok, 1.0, 0.0)
        at = ice_ref[jnp.clip(gx + dx, 0, GX - 1), jnp.clip(gy + dy, 0, GY - 1)]
        inside[dy, dx] = flag
        iced[dy, dx] = flag * at.astype(F32)

    def m(i, c):
        return 2 * (i + 1) + c

    def p(i):
        return 2 * (STRIP + 2) + 1 + i

    within = lane % 32
    block = lane // 32

    def region(i, table):
        base = jnp.full((8, 128), table[0, 0], F32)
        if i < HALO:
            return jnp.where(sub == 0, table[-1, 0], base)
        if i >= TILE + HALO - 7 * STRIP:
            return jnp.where(sub == 7, table[1, 0], base)
        return base

    def side_region(i, table):
        row = sub * STRIP + block * GROUP + i

        def by_row(dx):
            return jnp.where(
                row < HALO, table[-1, dx], jnp.where(row < HALO + TILE, table[0, dx], table[1, dx])
            )

        return jnp.where(within < HALO, by_row(1), by_row(-1))

    def shifts_of(t0, t1, x):
        w0 = [pltpu.roll(t, 1, 1) for t in t0]
        w1 = [pltpu.roll(t, 1, 1) for t in t1]
        e0 = [pltpu.roll(t, 127, 1) for t in t0]
        e1 = [pltpu.roll(t, 127, 1) for t in t1]
        wx = pltpu.roll(x, 1, 1)
        ex = pltpu.roll(x, 127, 1)
        west = [[], []]
        east = [[], []]
        west_x, east_x = wx, ex
        for g in range(4):
            from_x = wx if g == 3 else pltpu.roll(x, 97 - 32 * g, 1)
            west[0].append(jnp.where(lane == 0, from_x, w0[g]))
            west[1].append(jnp.where(lane == 0, w0[g], w1[g]))
            edge = w1[g] if g == 0 else pltpu.roll(t1[g], 32 * g + 1, 1)
            west_x = jnp.where(lane == 32 * g, edge, west_x)
            from_x = ex if g == 0 else pltpu.roll(x, 127 - 32 * g, 1)
            east[0].append(jnp.where(lane == 127, e1[g], e0[g]))
            east[1].append(jnp.where(lane == 127, from_x, e1[g]))
            edge = e0[g] if g == 3 else pltpu.roll(t0[g], 32 * g + 31, 1)
            east_x = jnp.where(lane == 32 * g + 31, edge, east_x)
        return east, east_x, west, west_x

    def keep_all(ref, i, t, x):
        for g in range(4):
            for c in range(2):
                ref[m(GROUP * g + i, c)] = t[c][g]
        ref[p(i)] = x

    def put(dst, i, u, ux, v, vx):
        for refs, t, x in ((dst[:3], u, ux), (dst[3:], v, vx)):
            east, east_x, west, west_x = shifts_of(t[0], t[1], x)
            keep_all(refs[0], i, t, x)
            keep_all(refs[1], i, east, east_x)
            keep_all(refs[2], i, west, west_x)

    def wrap(refs):
        for ref in refs:
            for c in range(2):
                ref[m(-1, c)] = pltpu.roll(ref[m(STRIP - 1, c)], 1, 0)
                ref[m(STRIP, c)] = pltpu.roll(ref[m(0, c)], 7, 0)
            y = pltpu.roll(ref[p(GROUP - 1)], 32, 1)
            ref[p(-1)] = jnp.where(lane < 32, pltpu.roll(y, 1, 0), y)
            y = pltpu.roll(ref[p(0)], 96, 1)
            ref[p(GROUP)] = jnp.where(lane >= 96, pltpu.roll(y, 7, 0), y)

    for h in halos[:2]:
        h.wait_recv()
    fields = (T, FU, FV, OU, OV)
    for i in range(STRIP):
        at = pl.ds(i, 8, stride=STRIP)
        for c in range(2):
            for f, dst in enumerate(fields):
                x = nat[f, c, at, :]
                if f == 0 and not HALO <= i < TILE + HALO - 7 * STRIP:
                    x = jnp.where(region(i, inside) > 0.0, x, 0.0)
                dst[m(i, c)] = x
    for h in halos[2:]:
        h.wait_recv()
    for ref in (h_west, h_east):
        ref[pl.ds(HALO + 128, 128)] = pltpu.roll(ref[pl.ds(HALO, 128)], 64, 1)
        ref[pl.ds(0, HALO)] = pltpu.roll(ref[pl.ds(0, HALO)], 64, 1)
    for i in range(GROUP):
        right = [h_east[pl.ds(GROUP * g + i, 8, stride=STRIP), :] for g in range(4)]
        left = [h_west[pl.ds(GROUP * g + i, 8, stride=STRIP), :] for g in range(4)]
        for f, dst in enumerate(fields):
            x = None
            for g in range(4):
                r = (32 * g - shifts[f]) % 128
                l = (32 * g + HALO - 112 + shifts[f]) % 128
                r = pltpu.roll(right[g], r, 1) if r else right[g]
                l = pltpu.roll(left[g], l, 1) if l else left[g]
                y = jnp.where(within < HALO, r, l)
                x = y if x is None else jnp.where(block == g, y, x)
            if f == 0:
                x = jnp.where(side_region(i, inside) > 0.0, x, 0.0)
            dst[p(i)] = x
    base = float(visc_scale * np.power(strain_floor, -1.0 / 3.0))
    every = [[m(GROUP * g + i, c) for c in range(2) for g in range(4)] + [p(i)] for i in range(GROUP)]

    def step_of(at, by):
        return at + 2 * by if at < p(-1) else at + by

    def split(values):
        return [values[:4], values[4:8]], values[8]

    def viscosity(src):
        for spot, i in enumerate([0, GROUP - 1] + list(range(1, GROUP - 1))):
            values = []
            for at in every[i]:
                if src is None:
                    values.append((0.5 * base) * T[at])
                    continue
                U, UE, UW, V, VE, VW = src
                ux = 0.5 * (UE[at] - UW[at])
                vx = 0.5 * (VE[at] - VW[at])
                uy = 0.5 * (U[step_of(at, 1)] - U[step_of(at, -1)])
                vy = 0.5 * (V[step_of(at, 1)] - V[step_of(at, -1)])
                sh = uy + vx
                strain = ux * ux + vy * vy + ux * vy + 0.25 * (sh * sh) + strain_floor
                values.append((0.5 * visc_scale) * T[at] * jnp.exp2(jnp.log2(strain) * (-1.0 / 3.0)))
            t, x = split(values)
            east, east_x, west, west_x = shifts_of(t[0], t[1], x)
            keep_all(H, i, t, x)
            keep_all(A, i, east, east_x)
            keep_all(B, i, west, west_x)
            if spot == 1:
                wrap([H])

    def sweep(src, dst, fu_ref, fv_ref, fresh, final=None):
        starts = list(range(0, GROUP, ROWS))
        for spot, s in enumerate([starts[0], starts[-1]] + starts[1:-1]):
            new_u = [[None] * 9 for _ in range(ROWS)]
            new_v = [[None] * 9 for _ in range(ROWS)]
            n = ROWS + 2
            for lot in range(8 if final is not None else 9):
                spots = [step_of(every[s][lot], j - 1) for j in range(n)]
                h = [H[at] for at in spots]
                face = [h[j] + h[j + 1] for j in range(n - 1)]
                if src is not None:
                    u, ue, uw, v, ve, vw = ([ref[at] for at in spots] for ref in src)
                    q = [h[j] * (ve[j] - vw[j]) for j in range(n)]
                    r = [h[j] * (ue[j] - uw[j]) for j in range(n)]
                for k in range(ROWS):
                    j = k + 1
                    at = spots[j]
                    a = A[at]
                    w_ = B[at]
                    fe = h[j] + a
                    fw = h[j] + w_
                    so = face[j]
                    no = face[j - 1]
                    if fresh:
                        ew = fe + fw
                        sn = so + no
                        step = s + k
                        if lot < 8:
                            step = GROUP * (lot % 4) + step
                            fr = FR[2 * (step // 4) + lot // 4]
                            ice = region(step, iced)
                        else:
                            fr = FR[2 * GROUP + step]
                            ice = IC[step]
                        iu = ice / (fr + 4.0 * ew + sn)
                        iv = ice / (fr + ew + 4.0 * sn)
                        IU[at] = iu
                        IV[at] = iv
                    else:
                        iu = IU[at]
                        iv = IV[at]
                    fu = fu_ref[at]
                    fv = fv_ref[at]
                    if src is not None:
                        cu = a * (ve[j + 1] - ve[j - 1]) - w_ * (vw[j + 1] - vw[j - 1]) + 0.5 * (q[j + 1] - q[j - 1])
                        cv = 0.5 * (a * (ue[j + 1] - ue[j - 1]) - w_ * (uw[j + 1] - uw[j - 1])) + (r[j + 1] - r[j - 1])
                        tu = fe * ue[j] + fw * uw[j]
                        su = so * u[j + 1] + no * u[j - 1]
                        tv = fe * ve[j] + fw * vw[j]
                        sv = so * v[j + 1] + no * v[j - 1]
                        fu = fu + 4.0 * tu + su + cu
                        fv = fv + tv + 4.0 * sv + cv
                    new_u[k][lot] = iu * fu
                    new_v[k][lot] = iv * fv
            if final is not None:
                for k in range(ROWS):
                    for lot in range(8):
                        at = every[s + k][lot]
                        final[at] = FU[at] * new_u[k][lot] + FV[at] * new_v[k][lot]
                continue
            for k in range(ROWS):
                put(dst, s + k, *split(new_u[k]), *split(new_v[k]))
            if spot == 1:
                wrap(dst)

    zero = (U0, UE0, UW0, V0, VE0, VW0)
    one = (U1, UE1, UW1, V1, VE1, VW1)
    viscosity(None)

    for g in gathers:
        g.wait_recv()

    def heard(dy, dx):
        return lax.rem(gy - tile(dy, dx) // 4 + GY, GY)

    both = jnp.where(eastern, c_recv[heard(0, 1), pl.ds(32, 8)], c_recv[heard(0, -1), pl.ds(32, 8)])
    for g, dx in enumerate((0, 1, -1)):
        row = 0 if dx == 0 else 4
        coarse[g, pl.ds(0, 2)] = c_recv[heard(-1, dx), pl.ds(40, 8)][row:row + 2]
        coarse[g, pl.ds(34, 2)] = c_recv[heard(1, dx), pl.ds(40, 8)][row + 2:row + 4]
        coarse[g, pl.ds(36, 4)] = jnp.zeros((4, 128), F32)
        if dx == 0:
            coarse[g, pl.ds(2, 32)] = c_recv[heard(0, 0), pl.ds(0, 32)]
        else:
            for q in range(4):
                shift = (128 - 4 * q if dx == 1 else 4 * q) % 128
                coarse[g, pl.ds(2 + 8 * q, 8)] = pltpu.roll(both, shift, 1) if shift else both
        flat = jnp.exp(coarse[g])
        cext[g, pl.ds(0, 40, stride=2), :] = flat
        cext[g, pl.ds(1, 40, stride=2), :] = pltpu.roll(flat, 64, 1)
    quarter = lane // 4
    sides = []
    for i in range(GROUP):
        at = pl.ds(i, 8, stride=GROUP)
        mid, right, left = (cext[g, at, :] for g in range(3))
        edges = jnp.where(lane < 64, right, pltpu.roll(left, 64, 1))
        FR[2 * i] = jnp.take_along_axis(mid, quarter, axis=1)
        FR[2 * i + 1] = jnp.take_along_axis(mid, quarter + 32, axis=1)
        sides.append(
            jnp.take_along_axis(edges, jnp.where(within < HALO, within // 4, 120 + within // 4), axis=1)
        )
    for i in range(GROUP):
        x = sides[i // 4]
        for g in range(1, 4):
            x = jnp.where(block == g, sides[(GROUP * g + i) // 4], x)
        FR[2 * GROUP + i] = x
        IC[i] = side_region(i, iced)

    sweep(None, one, FU, FV, True)
    sweep(one, zero, FU, FV, False)

    @pl.loop(1, PIC)
    def _(_):
        viscosity(zero)
        sweep(zero, one, FU, FV, True)
        sweep(one, zero, FU, FV, False)

    for i in range(GROUP):
        new_u, new_v = [], []
        for at in every[i]:
            u = U0[at]
            v = V0[at]
            FU[at] = u
            FV[at] = v
            mu = u - OU[at]
            mv = v - OV[at]
            OU[at] = mu
            OV[at] = mv
            new_u.append(IU[at] * mu)
            new_v.append(IV[at] * mv)
        put(one, i, *split(new_u), *split(new_v))
    for h in halos:
        h.wait_send()
    for i in range(STRIP):
        at = pl.ds(i, 8, stride=STRIP)
        for c in range(2):
            nat[0, c, at, :] = FU[m(i, c)]
            nat[1, c, at, :] = FV[m(i, c)]

    stores = []
    for f, dst in enumerate((out_u, out_v)):
        for c in range(2):
            stores.append(
                pltpu.make_async_copy(nat.at[f, c, inner], dst.at[:, pl.ds(c * 128, 128)], o_sem.at[f, c])
            )
    for s in stores:
        s.start()
    wrap(one)

    @pl.loop(0, (ADJ - 2) // 2)
    def _(_):
        sweep(one, zero, OU, OV, False)
        sweep(zero, one, OU, OV, False)

    sweep(one, zero, OU, OV, False, final=T)

    for i in range(GROUP):
        total = None
        for k in range(4):
            j = i * 4 + k
            cell = [T[m(j, c)] for c in range(2)]
            total = cell if total is None else [total[c] + cell[c] for c in range(2)]
        spots = []
        for c in range(2):
            x = -FR[2 * i + c] * total[c]
            x = x + pltpu.roll(x, 127, 1)
            x = x + pltpu.roll(x, 126, 1)
            spots.append(jnp.take_along_axis(x, (lane % 32) * 4, axis=1))
        both = jnp.where(lane % 64 < 32, spots[0], spots[1])
        small[pl.ds(i, 8, stride=GROUP), :] = both
    even = small[pl.ds(4, 32, stride=2), :]
    odd = small[pl.ds(5, 32, stride=2), :]
    wide = lax.broadcasted_iota(jnp.int32, (32, 128), 1)
    grad[...] = jnp.where(wide < 64, even, odd)

    first, second, third = [], [], []
    for g in range(GX):
        part[g] = grad[pl.ds(4 * g, 4), :]
    if REMOTE:
        first = [
            remote(part.at[lax.rem(gx + off, GX)], slots.at[off], b_send.at[off], b_recv.at[off], dev(0, off))
            for off in range(1, GX)
        ]
    for c in first:
        c.start()
    slots[0] = part[gx]
    owners = [blk[lax.rem(gx - off + GX, GX), 0, gy] for off in range(GX)]
    which = lax.broadcasted_iota(jnp.int32, (16, 128), 0) % 4
    for c in first:
        c.wait_recv()
    cells = []
    for t in range(GX):
        x = slots[t]
        cells.append(jnp.concatenate([jnp.broadcast_to(x[j:j + 1], (4, 128)) for j in range(4)], axis=0))
    if REMOTE:
        second = [
            remote(sums.at[off], tiles.at[off], a_send.at[off], a_recv.at[off], dev(off, 0)) for off in range(1, GY)
        ]
    for off in list(range(1, GY)) + [0]:
        lowest = 4 * lax.rem(gy + off, GY)
        total = jnp.zeros((16, 128), F32)
        for t in range(GX):
            total = total + jnp.where(which == owners[t] - lowest, cells[t], 0.0)
        sums[off] = total
        if off > 0 and REMOTE:
            second[off - 1].start()
    total = sums[0]
    for off in range(1, GY):
        if REMOTE:
            second[off - 1].wait_recv()
        total = total + tiles[off]
    red[...] = total
    if REMOTE:
        third = [
            remote(red, gathered.at[gx], d_send.at[off], d_recv.at[off], dev(0, off)) for off in range(1, GX)
        ]
    for c in third:
        c.start()
    gathered[gx] = total
    for c in third:
        c.wait_recv()
    for g in range(GX):
        for j in range(4):
            out_g[:, pl.ds((4 * g + j) * 128, 128)] = gathered[g, pl.ds(4 * j, 4)]
    for c in gathers + first + second + third:
        c.wait_send()
    for s in stores:
        s.wait()


def call(*operands):
    shape = jax.ShapeDtypeStruct
    dma = pltpu.SemaphoreType.DMA
    hbm = pl.BlockSpec(memory_space=pltpu.HBM)
    smem = pl.BlockSpec(memory_space=pltpu.SMEM)
    vmem = pl.BlockSpec(memory_space=pltpu.VMEM)
    field = pltpu.VMEM((2 * (STRIP + 2) + GROUP + 2, 8, 128), F32)
    flat = pltpu.VMEM((32, 128), F32)
    return pl.pallas_call(
        kernel,
        name="friction_gradient",
        out_shape=(shape((TILE, TILE), F32), shape((TILE, TILE), F32), shape((4, 4096), F32)),
        in_specs=[smem, smem, hbm, hbm, hbm, hbm],
        out_specs=[hbm, hbm, vmem],
        scratch_shapes=[
            pltpu.VMEM((5, 2, EXT, 128), F32),
            pltpu.VMEM((128, 128), F32),
            pltpu.VMEM((128, 128), F32),
            pltpu.VMEM((EXT, 128), F32),
            pltpu.VMEM((EXT, 128), F32),
            pltpu.VMEM((4, 4096), F32),
            pltpu.VMEM((4, 32, 128), F32),
            pltpu.VMEM((4, 8, 128), F32),
            pltpu.VMEM((4, 8, 128), F32),
            pltpu.VMEM((GY, 48, 128), F32),
            pltpu.VMEM((GY, 48, 128), F32),
            pltpu.VMEM((3, 40, 128), F32),
            pltpu.VMEM((3, 80, 128), F32),
            field, field, field, field, field,
            pltpu.VMEM((3 * GROUP, 8, 128), F32),
            pltpu.VMEM((GROUP, 8, 128), F32),
            field, field, field, field, field,
        ] + [field] * 12 + [
            pltpu.VMEM((72, 128), F32),
            flat,
            pltpu.VMEM((GY, 16, 128), F32),
            pltpu.VMEM((GY, 16, 128), F32),
            pltpu.VMEM((GX, 4, 128), F32),
            pltpu.VMEM((GX, 4, 128), F32),
            pltpu.VMEM((16, 128), F32),
            pltpu.VMEM((GX, 16, 128), F32),
            dma, dma((3, 2)), dma((2, 2)),
            dma((GY,)), dma((GY,)), dma((8,)), dma((8,)),
            dma((GY,)), dma((GY,)), dma((GX,)), dma((GX,)), dma((GX,)), dma((GX,)),
        ],
        compiler_params=pltpu.CompilerParams(
            vmem_limit_bytes=60 << 20,
            **(dict(collective_id=0, has_side_effects=True) if REMOTE else {}),
        ),
    )(*operands)


def per_device(thickness, driving, observed, control, ice_mask, tile_block):
    return call(
        tile_block.transpose(1, 2, 0), ice_mask.T, thickness, driving, observed, control
    )


def solution(mesh):
    return jax.shard_map(
        per_device,
        mesh=mesh,
        in_specs=(P("gy", "gx"), P(None, "gy", "gx"), P(None, "gy", "gx"), P("gy", None), P(), P()),
        out_specs=(P("gy", "gx"), P("gy", "gx"), P("gy", None)),
        check_vma=False,
    )
```

```python
import jax
import jax.numpy as jnp
import numpy as np
from jax import lax
from jax.experimental import pallas as pl
from jax.experimental.pallas import tpu as pltpu
from jax.sharding import PartitionSpec as P

TILE = 256
HALO = 16
EXT = TILE + 2 * HALO
STRIP = EXT // 8
GROUP = STRIP // 4
PIC = 4
ADJ = 6
GX = 8
GY = 16
ROWS = 3
PARTS = 2
REMOTE = True
MESH = pl.DeviceIdType.MESH
F32 = jnp.float32

visc_scale = 0.1
strain_floor = 0.05


def kernel(
    blk, ice_ref, thick, drv, obs, ctl,
    out_u, out_v, out_g,
    nat, pack_w, pack_e, h_west, h_east, c_in, c_own, c_side, c_ends, c_send, c_recv, coarse, cext,
    T, FU, FV, OU, OV, FR, IC, H, A, B, IU, IV,
    U0, UE0, UW0, V0, VE0, VW0, U1, UE1, UW1, V1, VE1, VW1,
    small, grad, sums, tiles, part, slots, red, gathered,
    k_sem, l_sem, o_sem, g_send, g_recv, x_send, x_recv,
    a_send, a_recv, b_send, b_recv, d_send, d_recv,
):
    gx = lax.axis_index("gx")
    gy = lax.axis_index("gy")

    def dev(dy, dx):
        return (lax.rem(gx + dx + GX, GX), lax.rem(gy + dy + GY, GY))

    def remote(src, dst, ss, rs, to):
        return pltpu.make_async_remote_copy(
            src_ref=src, dst_ref=dst, send_sem=ss, recv_sem=rs, device_id=to, device_id_type=MESH
        )

    rates = pltpu.make_async_copy(ctl, c_in, k_sem)
    rates.start()
    near = [(dy, dx) for dy in (-1, 0, 1) for dx in (-1, 0, 1) if (dy, dx) != (0, 0)]
    if REMOTE:
        barrier = pltpu.get_barrier_semaphore()
        peers = [(dy, 0) for dy in range(1, GY)] + [(0, dx) for dx in range(1, GX)]
        peers += [(dy, dx) for dy, dx in near if dy * dx]
        for dy, dx in peers:
            pl.semaphore_signal(barrier, inc=1, device_id=dev(dy, dx), device_id_type=MESH)

    inner = pl.ds(HALO, TILE)
    loads = []
    for c in range(2):
        cols = pl.ds(c * 128, 128)
        loads.append(pltpu.make_async_copy(thick.at[:, cols], nat.at[0, c, inner], l_sem.at[0, c]))
        loads.append(pltpu.make_async_copy(drv.at[:, :, cols], nat.at[pl.ds(1, 2), c, inner], l_sem.at[1, c]))
        loads.append(pltpu.make_async_copy(obs.at[:, :, cols], nat.at[pl.ds(3, 2), c, inner], l_sem.at[2, c]))
    for copy in loads:
        copy.start()

    lane = lax.broadcasted_iota(jnp.int32, (8, 128), 1)
    sub = lax.broadcasted_iota(jnp.int32, (8, 128), 0)

    rates.wait()
    for t in range(32):
        x = c_in[:, pl.ds(t * 128, 128)]
        for k in range(4):
            c_own[k, pl.ds(t, 1)] = x[k:k + 1]
    for k in range(4):
        for g in range(4):
            x = c_own[k, pl.ds(8 * g, 8)]
            right = pltpu.roll(x, 4 * g, 1) if g else x
            left = pltpu.roll(x, 128 - 4 * g, 1) if g else x
            if g == 0:
                side = x
            else:
                side = jnp.where((lane % 64 >= 4 * g) & (lane % 64 < 32), right, side)
                side = jnp.where((lane % 64 >= 32) & (lane % 64 < 64 - 4 * g), left, side)
        c_side[k] = side
        for half in range(2):
            c_ends[k, pl.ds(4 * half, 2)] = c_own[k, pl.ds(30, 2)]
            c_ends[k, pl.ds(4 * half + 2, 2)] = c_own[k, pl.ds(0, 2)]
    eastern = lane % 64 < 32

    seen = [
        [blk[lax.rem(gx + dx + GX, GX), 0, lax.rem(gy + dy, GY)] for dy in range(GY)] for dx in (-1, 0, 1)
    ]

    def tile(dy, dx):
        return seen[dx + 1][dy % GY]

    gathers = []
    if REMOTE:
        pl.semaphore_wait(barrier, len(peers))
        gathers = [
            remote(c_send.at[off], c_recv.at[off], g_send.at[off], g_recv.at[off], dev(off, 0))
            for off in range(1, GY)
        ]
    for off in list(range(1, GY)) + [0]:
        pick = {
            (dy, dx): tile(off + dy, dx) & 3 for dy in (-1, 0, 1) for dx in (-1, 0, 1)
        }
        c_send[off, pl.ds(0, 32)] = c_own[pick[0, 0]]
        c_send[off, pl.ds(32, 8)] = jnp.where(eastern, c_side[pick[0, 1]], c_side[pick[0, -1]])
        corner_n = jnp.where(eastern, c_ends[pick[-1, 1]], c_ends[pick[-1, -1]])
        corner_s = jnp.where(eastern, c_ends[pick[1, 1]], c_ends[pick[1, -1]])
        ends = jnp.where(sub < 2, c_ends[pick[-1, 0]], c_ends[pick[1, 0]])
        c_send[off, pl.ds(40, 8)] = jnp.where(sub < 4, ends, jnp.where(sub < 6, corner_n, corner_s))
        if off > 0 and REMOTE:
            gathers[off - 1].start()
    c_recv[0] = c_send[0]

    for copy in loads:
        copy.wait()

    def send(at, moves):
        copies = [
            remote(s, d, x_send.at[at + n], x_recv.at[at + n], dev(*to)) for n, (s, d, to) in enumerate(moves)
        ]
        for c in copies:
            c.start()
        return copies

    halos = []
    first, last = pl.ds(0, HALO), pl.ds(TILE + HALO, HALO)
    if REMOTE:
        halos += send(0, [
            (nat.at[:, :, pl.ds(TILE, HALO)], nat.at[:, :, first], (1, 0)),
            (nat.at[:, :, pl.ds(HALO, HALO)], nat.at[:, :, last], (-1, 0)),
        ])
    shifts = (0, 16, 32, 48, 56)
    for t in range(16):
        w = e = None
        for half in range(2):
            at = pl.ds(HALO + half * 128 + t * 8, 8)
            for f in range(5):
                shift = shifts[f] + 64 * half
                x = nat[f, 0, at]
                y = nat[f, 1, at]
                if shift:
                    x = pltpu.roll(x, shift, 1)
                    y = pltpu.roll(y, 128 - shift, 1)
                w = x if w is None else jnp.where(lane < shift, w, x)
                e = y if e is None else jnp.where(lane >= 128 - shift, e, y)
        pack_w[pl.ds(t * 8, 8), :] = w
        pack_e[pl.ds(t * 8, 8), :] = e

    if REMOTE:
        half = pl.ds(HALO, 128)
        head, tail = pl.ds(0, HALO), pl.ds(112, HALO)
        halos += send(2, [
            (pack_e, h_west.at[half], (0, 1)),
            (pack_w, h_east.at[half], (0, -1)),
            (pack_e.at[tail], h_west.at[first], (1, 1)),
            (pack_e.at[head], h_west.at[last], (-1, 1)),
            (pack_w.at[tail], h_east.at[first], (1, -1)),
            (pack_w.at[head], h_east.at[last], (-1, -1)),
        ])

    inside, iced = {}, {}
    for dy, dx in near + [(0, 0)]:
        ok = (gy + dy >= 0) & (gy + dy < GY) & (gx + dx >= 0) & (gx + dx < GX)
        flag = jnp.where(ok, 1.0, 0.0)
        at = ice_ref[jnp.clip(gx + dx, 0, GX - 1), jnp.clip(gy + dy, 0, GY - 1)]
        inside[dy, dx] = flag
        iced[dy, dx] = flag * at.astype(F32)

    def m(i, c):
        return 2 * (i + 1) + c

    def p(i):
        return 2 * (STRIP + 2) + 1 + i

    within = lane % 32
    block = lane // 32

    def region(i, table):
        base = jnp.full((8, 128), table[0, 0], F32)
        if i < HALO:
            return jnp.where(sub == 0, table[-1, 0], base)
        if i >= TILE + HALO - 7 * STRIP:
            return jnp.where(sub == 7, table[1, 0], base)
        return base

    def side_region(i, table):
        row = sub * STRIP + block * GROUP + i

        def by_row(dx):
            return jnp.where(
                row < HALO, table[-1, dx], jnp.where(row < HALO + TILE, table[0, dx], table[1, dx])
            )

        return jnp.where(within < HALO, by_row(1), by_row(-1))

    def shifts_of(t0, t1, x):
        w0 = [pltpu.roll(t, 1, 1) for t in t0]
        w1 = [pltpu.roll(t, 1, 1) for t in t1]
        e0 = [pltpu.roll(t, 127, 1) for t in t0]
        e1 = [pltpu.roll(t, 127, 1) for t in t1]
        wx = pltpu.roll(x, 1, 1)
        ex = pltpu.roll(x, 127, 1)
        west = [[], []]
        east = [[], []]
        west_x, east_x = wx, ex
        for g in range(4):
            from_x = wx if g == 3 else pltpu.roll(x, 97 - 32 * g, 1)
            west[0].append(jnp.where(lane == 0, from_x, w0[g]))
            west[1].append(jnp.where(lane == 0, w0[g], w1[g]))
            edge = w1[g] if g == 0 else pltpu.roll(t1[g], 32 * g + 1, 1)
            west_x = jnp.where(lane == 32 * g, edge, west_x)
            from_x = ex if g == 0 else pltpu.roll(x, 127 - 32 * g, 1)
            east[0].append(jnp.where(lane == 127, e1[g], e0[g]))
            east[1].append(jnp.where(lane == 127, from_x, e1[g]))
            edge = e0[g] if g == 3 else pltpu.roll(t0[g], 32 * g + 31, 1)
            east_x = jnp.where(lane == 32 * g + 31, edge, east_x)
        return east, east_x, west, west_x

    def keep_all(ref, i, t, x):
        for g in range(4):
            for c in range(2):
                ref[m(GROUP * g + i, c)] = t[c][g]
        ref[p(i)] = x

    def put(dst, i, u, ux, v, vx):
        for refs, t, x in ((dst[:3], u, ux), (dst[3:], v, vx)):
            east, east_x, west, west_x = shifts_of(t[0], t[1], x)
            keep_all(refs[0], i, t, x)
            keep_all(refs[1], i, east, east_x)
            keep_all(refs[2], i, west, west_x)

    def wrap(refs):
        for ref in refs:
            for c in range(2):
                ref[m(-1, c)] = pltpu.roll(ref[m(STRIP - 1, c)], 1, 0)
                ref[m(STRIP, c)] = pltpu.roll(ref[m(0, c)], 7, 0)
            y = pltpu.roll(ref[p(GROUP - 1)], 32, 1)
            ref[p(-1)] = jnp.where(lane < 32, pltpu.roll(y, 1, 0), y)
            y = pltpu.roll(ref[p(0)], 96, 1)
            ref[p(GROUP)] = jnp.where(lane >= 96, pltpu.roll(y, 7, 0), y)

    for h in halos[:2]:
        h.wait_recv()
    fields = (T, FU, FV, OU, OV)
    for i in range(STRIP):
        at = pl.ds(i, 8, stride=STRIP)
        for c in range(2):
            for f, dst in enumerate(fields):
                x = nat[f, c, at, :]
                if f == 0 and not HALO <= i < TILE + HALO - 7 * STRIP:
                    x = jnp.where(region(i, inside) > 0.0, x, 0.0)
                dst[m(i, c)] = x
    for h in halos[2:]:
        h.wait_recv()
    for ref in (h_west, h_east):
        ref[pl.ds(HALO + 128, 128)] = pltpu.roll(ref[pl.ds(HALO, 128)], 64, 1)
        ref[pl.ds(0, HALO)] = pltpu.roll(ref[pl.ds(0, HALO)], 64, 1)
    for i in range(GROUP):
        right = [h_east[pl.ds(GROUP * g + i, 8, stride=STRIP), :] for g in range(4)]
        left = [h_west[pl.ds(GROUP * g + i, 8, stride=STRIP), :] for g in range(4)]
        for f, dst in enumerate(fields):
            x = None
            for g in range(4):
                r = (32 * g - shifts[f]) % 128
                l = (32 * g + HALO - 112 + shifts[f]) % 128
                r = pltpu.roll(right[g], r, 1) if r else right[g]
                l = pltpu.roll(left[g], l, 1) if l else left[g]
                y = jnp.where(within < HALO, r, l)
                x = y if x is None else jnp.where(block == g, y, x)
            if f == 0:
                x = jnp.where(side_region(i, inside) > 0.0, x, 0.0)
            dst[p(i)] = x
    base = float(visc_scale * np.power(strain_floor, -1.0 / 3.0))
    every = [[m(GROUP * g + i, c) for c in range(2) for g in range(4)] + [p(i)] for i in range(GROUP)]

    def step_of(at, by):
        return at + 2 * by if at < p(-1) else at + by

    def split(values):
        return [values[:4], values[4:8]], values[8]

    def viscosity(src):
        for spot, i in enumerate([0, GROUP - 1] + list(range(1, GROUP - 1))):
            values = []
            for at in every[i]:
                if src is None:
                    values.append((0.5 * base) * T[at])
                    continue
                U, UE, UW, V, VE, VW = src
                ux = 0.5 * (UE[at] - UW[at])
                vx = 0.5 * (VE[at] - VW[at])
                uy = 0.5 * (U[step_of(at, 1)] - U[step_of(at, -1)])
                vy = 0.5 * (V[step_of(at, 1)] - V[step_of(at, -1)])
                sh = uy + vx
                strain = ux * ux + vy * vy + ux * vy + 0.25 * (sh * sh) + strain_floor
                values.append((0.5 * visc_scale) * T[at] * jnp.exp2(jnp.log2(strain) * (-1.0 / 3.0)))
            t, x = split(values)
            east, east_x, west, west_x = shifts_of(t[0], t[1], x)
            keep_all(H, i, t, x)
            keep_all(A, i, east, east_x)
            keep_all(B, i, west, west_x)
            if spot == 1:
                wrap([H])

    def sweep(src, dst, fu_ref, fv_ref, fresh, final=None):
        starts = list(range(0, GROUP, ROWS))
        for spot, s in enumerate([starts[0], starts[-1]] + starts[1:-1]):
            new_u = [[None] * 9 for _ in range(ROWS)]
            new_v = [[None] * 9 for _ in range(ROWS)]
            n = ROWS + 2
            for lot in range(8 if final is not None else 9):
                spots = [step_of(every[s][lot], j - 1) for j in range(n)]
                h = [H[at] for at in spots]
                face = [h[j] + h[j + 1] for j in range(n - 1)]
                if src is not None:
                    u, ue, uw, v, ve, vw = ([ref[at] for at in spots] for ref in src)
                    q = [h[j] * (ve[j] - vw[j]) for j in range(n)]
                    r = [h[j] * (ue[j] - uw[j]) for j in range(n)]
                for k in range(ROWS):
                    j = k + 1
                    at = spots[j]
                    a = A[at]
                    w_ = B[at]
                    fe = h[j] + a
                    fw = h[j] + w_
                    so = face[j]
                    no = face[j - 1]
                    if fresh:
                        ew = fe + fw
                        sn = so + no
                        step = s + k
                        if lot < 8:
                            step = GROUP * (lot % 4) + step
                            fr = FR[2 * (step // 4) + lot // 4]
                            ice = region(step, iced)
                        else:
                            fr = FR[2 * GROUP + step]
                            ice = IC[step]
                        iu = ice / (fr + 4.0 * ew + sn)
                        iv = ice / (fr + ew + 4.0 * sn)
                        IU[at] = iu
                        IV[at] = iv
                    else:
                        iu = IU[at]
                        iv = IV[at]
                    fu = fu_ref[at]
                    fv = fv_ref[at]
                    if src is not None:
                        cu = a * (ve[j + 1] - ve[j - 1]) - w_ * (vw[j + 1] - vw[j - 1]) + 0.5 * (q[j + 1] - q[j - 1])
                        cv = 0.5 * (a * (ue[j + 1] - ue[j - 1]) - w_ * (uw[j + 1] - uw[j - 1])) + (r[j + 1] - r[j - 1])
                        tu = fe * ue[j] + fw * uw[j]
                        su = so * u[j + 1] + no * u[j - 1]
                        tv = fe * ve[j] + fw * vw[j]
                        sv = so * v[j + 1] + no * v[j - 1]
                        fu = fu + 4.0 * tu + su + cu
                        fv = fv + tv + 4.0 * sv + cv
                    new_u[k][lot] = iu * fu
                    new_v[k][lot] = iv * fv
            if final is not None:
                for k in range(ROWS):
                    for lot in range(8):
                        at = every[s + k][lot]
                        final[at] = FU[at] * new_u[k][lot] + FV[at] * new_v[k][lot]
                continue
            for k in range(ROWS):
                put(dst, s + k, *split(new_u[k]), *split(new_v[k]))
            if spot == 1:
                wrap(dst)

    zero = (U0, UE0, UW0, V0, VE0, VW0)
    one = (U1, UE1, UW1, V1, VE1, VW1)
    viscosity(None)

    for g in gathers:
        g.wait_recv()

    def heard(dy, dx):
        return lax.rem(gy - tile(dy, dx) // 4 + GY, GY)

    both = jnp.where(eastern, c_recv[heard(0, 1), pl.ds(32, 8)], c_recv[heard(0, -1), pl.ds(32, 8)])
    for g, dx in enumerate((0, 1, -1)):
        row = 0 if dx == 0 else 4
        coarse[g, pl.ds(0, 2)] = c_recv[heard(-1, dx), pl.ds(40, 8)][row:row + 2]
        coarse[g, pl.ds(34, 2)] = c_recv[heard(1, dx), pl.ds(40, 8)][row + 2:row + 4]
        coarse[g, pl.ds(36, 4)] = jnp.zeros((4, 128), F32)
        if dx == 0:
            coarse[g, pl.ds(2, 32)] = c_recv[heard(0, 0), pl.ds(0, 32)]
        else:
            for q in range(4):
                shift = (128 - 4 * q if dx == 1 else 4 * q) % 128
                coarse[g, pl.ds(2 + 8 * q, 8)] = pltpu.roll(both, shift, 1) if shift else both
        flat = jnp.exp(coarse[g])
        cext[g, pl.ds(0, 40, stride=2), :] = flat
        cext[g, pl.ds(1, 40, stride=2), :] = pltpu.roll(flat, 64, 1)
    quarter = lane // 4
    sides = []
    for i in range(GROUP):
        at = pl.ds(i, 8, stride=GROUP)
        mid, right, left = (cext[g, at, :] for g in range(3))
        edges = jnp.where(lane < 64, right, pltpu.roll(left, 64, 1))
        FR[2 * i] = jnp.take_along_axis(mid, quarter, axis=1)
        FR[2 * i + 1] = jnp.take_along_axis(mid, quarter + 32, axis=1)
        sides.append(
            jnp.take_along_axis(edges, jnp.where(within < HALO, within // 4, 120 + within // 4), axis=1)
        )
    for i in range(GROUP):
        x = sides[i // 4]
        for g in range(1, 4):
            x = jnp.where(block == g, sides[(GROUP * g + i) // 4], x)
        FR[2 * GROUP + i] = x
        IC[i] = side_region(i, iced)

    sweep(None, one, FU, FV, True)
    sweep(one, zero, FU, FV, False)

    @pl.loop(1, PIC)
    def _(_):
        viscosity(zero)
        sweep(zero, one, FU, FV, True)
        sweep(one, zero, FU, FV, False)

    for i in range(GROUP):
        new_u, new_v = [], []
        for at in every[i]:
            u = U0[at]
            v = V0[at]
            FU[at] = u
            FV[at] = v
            mu = u - OU[at]
            mv = v - OV[at]
            OU[at] = mu
            OV[at] = mv
            new_u.append(IU[at] * mu)
            new_v.append(IV[at] * mv)
        put(one, i, *split(new_u), *split(new_v))
    for h in halos:
        h.wait_send()
    for i in range(STRIP):
        at = pl.ds(i, 8, stride=STRIP)
        for c in range(2):
            nat[0, c, at, :] = FU[m(i, c)]
            nat[1, c, at, :] = FV[m(i, c)]

    stores = []
    for f, dst in enumerate((out_u, out_v)):
        for c in range(2):
            stores.append(
                pltpu.make_async_copy(nat.at[f, c, inner], dst.at[:, pl.ds(c * 128, 128)], o_sem.at[f, c])
            )
    for s in stores:
        s.start()
    wrap(one)

    @pl.loop(0, (ADJ - 2) // 2)
    def _(_):
        sweep(one, zero, OU, OV, False)
        sweep(zero, one, OU, OV, False)

    sweep(one, zero, OU, OV, False, final=T)

    for i in range(GROUP):
        total = None
        for k in range(4):
            j = i * 4 + k
            cell = [T[m(j, c)] for c in range(2)]
            total = cell if total is None else [total[c] + cell[c] for c in range(2)]
        spots = []
        for c in range(2):
            x = -FR[2 * i + c] * total[c]
            x = x + pltpu.roll(x, 127, 1)
            x = x + pltpu.roll(x, 126, 1)
            spots.append(jnp.take_along_axis(x, (lane % 32) * 4, axis=1))
        both = jnp.where(lane % 64 < 32, spots[0], spots[1])
        small[pl.ds(i, 8, stride=GROUP), :] = both
    even = small[pl.ds(4, 32, stride=2), :]
    odd = small[pl.ds(5, 32, stride=2), :]
    wide = lax.broadcasted_iota(jnp.int32, (32, 128), 1)
    grad[...] = jnp.where(wide < 64, even, odd)

    first, second, third = [], [], []
    for g in range(GX):
        part[g] = grad[pl.ds(4 * g, 4), :]
    if REMOTE:
        first = [
            remote(part.at[lax.rem(gx + off, GX)], slots.at[off], b_send.at[off], b_recv.at[off], dev(0, off))
            for off in range(1, GX)
        ]
    for c in first:
        c.start()
    slots[0] = part[gx]
    owners = [blk[lax.rem(gx - off + GX, GX), 0, gy] for off in range(GX)]
    which = lax.broadcasted_iota(jnp.int32, (16, 128), 0) % 4
    for c in first:
        c.wait_recv()
    cells = []
    for t in range(GX):
        x = slots[t]
        cells.append(jnp.concatenate([jnp.broadcast_to(x[j:j + 1], (4, 128)) for j in range(4)], axis=0))
    if REMOTE:
        second = [
            remote(sums.at[off], tiles.at[off], a_send.at[off], a_recv.at[off], dev(off, 0)) for off in range(1, GY)
        ]
    for off in list(range(1, GY)) + [0]:
        lowest = 4 * lax.rem(gy + off, GY)
        total = jnp.zeros((16, 128), F32)
        for t in range(GX):
            total = total + jnp.where(which == owners[t] - lowest, cells[t], 0.0)
        sums[off] = total
        if off > 0 and REMOTE:
            second[off - 1].start()
    total = sums[0]
    for off in range(1, GY):
        if REMOTE:
            second[off - 1].wait_recv()
        total = total + tiles[off]
    red[...] = total
    if REMOTE:
        third = [
            remote(red, gathered.at[gx], d_send.at[off], d_recv.at[off], dev(0, off)) for off in range(1, GX)
        ]
    for c in third:
        c.start()
    gathered[gx] = total
    for c in third:
        c.wait_recv()
    for g in range(GX):
        for j in range(4):
            out_g[:, pl.ds((4 * g + j) * 128, 128)] = gathered[g, pl.ds(4 * j, 4)]
    for c in gathers + first + second + third:
        c.wait_send()
    for s in stores:
        s.wait()


def call(*operands):
    shape = jax.ShapeDtypeStruct
    dma = pltpu.SemaphoreType.DMA
    hbm = pl.BlockSpec(memory_space=pltpu.HBM)
    smem = pl.BlockSpec(memory_space=pltpu.SMEM)
    vmem = pl.BlockSpec(memory_space=pltpu.VMEM)
    field = pltpu.VMEM((2 * (STRIP + 2) + GROUP + 2, 8, 128), F32)
    flat = pltpu.VMEM((32, 128), F32)
    return pl.pallas_call(
        kernel,
        name="friction_gradient",
        out_shape=(shape((TILE, TILE), F32), shape((TILE, TILE), F32), shape((4, 4096), F32)),
        in_specs=[smem, smem, hbm, hbm, hbm, hbm],
        out_specs=[hbm, hbm, vmem],
        scratch_shapes=[
            pltpu.VMEM((5, 2, EXT, 128), F32),
            pltpu.VMEM((128, 128), F32),
            pltpu.VMEM((128, 128), F32),
            pltpu.VMEM((EXT, 128), F32),
            pltpu.VMEM((EXT, 128), F32),
            pltpu.VMEM((4, 4096), F32),
            pltpu.VMEM((4, 32, 128), F32),
            pltpu.VMEM((4, 8, 128), F32),
            pltpu.VMEM((4, 8, 128), F32),
            pltpu.VMEM((GY, 48, 128), F32),
            pltpu.VMEM((GY, 48, 128), F32),
            pltpu.VMEM((3, 40, 128), F32),
            pltpu.VMEM((3, 80, 128), F32),
            field, field, field, field, field,
            pltpu.VMEM((3 * GROUP, 8, 128), F32),
            pltpu.VMEM((GROUP, 8, 128), F32),
            field, field, field, field, field,
        ] + [field] * 12 + [
            pltpu.VMEM((72, 128), F32),
            flat,
            pltpu.VMEM((GY, 16, 128), F32),
            pltpu.VMEM((GY, 16, 128), F32),
            pltpu.VMEM((GX, 4, 128), F32),
            pltpu.VMEM((GX, 4, 128), F32),
            pltpu.VMEM((16, 128), F32),
            pltpu.VMEM((GX, 16, 128), F32),
            dma, dma((3, 2)), dma((2, 2)),
            dma((GY,)), dma((GY,)), dma((8,)), dma((8,)),
            dma((GY,)), dma((GY,)), dma((GX,)), dma((GX,)), dma((GX,)), dma((GX,)),
        ],
        compiler_params=pltpu.CompilerParams(
            vmem_limit_bytes=60 << 20,
            **(dict(collective_id=0, has_side_effects=True) if REMOTE else {}),
        ),
    )(*operands)


def copy_kernel(u, v, g, out_u, out_v, out_g, via, via_g, sem_in, sem_out):
    part = TILE // PARTS
    moves = []
    for n, (src, dst) in enumerate(((u, out_u), (v, out_v))):
        for k in range(PARTS):
            rows = pl.ds(k * part, part)
            moves.append((src.at[rows], via.at[n, rows], dst.at[rows]))
    moves.append((g, via_g, out_g))
    into = [pltpu.make_async_copy(a, b, sem_in.at[n]) for n, (a, b, _) in enumerate(moves)]
    out = [pltpu.make_async_copy(b, c, sem_out.at[n]) for n, (_, b, c) in enumerate(moves)]
    for c in into:
        c.start()
    for a, b in zip(into, out):
        a.wait()
        b.start()
    for c in out:
        c.wait()


def hand_out(*arrays):
    hbm = pl.BlockSpec(memory_space=pltpu.HBM)
    return pl.pallas_call(
        copy_kernel,
        name="hand_out",
        out_shape=tuple(jax.ShapeDtypeStruct(a.shape, F32) for a in arrays),
        in_specs=[hbm] * 3,
        out_specs=[hbm] * 3,
        scratch_shapes=[
            pltpu.VMEM((2, TILE, TILE), F32),
            pltpu.VMEM((4, 4096), F32),
            pltpu.SemaphoreType.DMA((2 * PARTS + 1,)),
            pltpu.SemaphoreType.DMA((2 * PARTS + 1,)),
        ],
        compiler_params=pltpu.CompilerParams(vmem_limit_bytes=60 << 20),
    )(*arrays)


def per_device(thickness, driving, observed, control, ice_mask, tile_block):
    results = call(
        tile_block.transpose(1, 2, 0), ice_mask.T, thickness, driving, observed, control
    )
    return hand_out(*results)


def solution(mesh):
    return jax.shard_map(
        per_device,
        mesh=mesh,
        in_specs=(P("gy", "gx"), P(None, "gy", "gx"), P(None, "gy", "gx"), P("gy", None), P(), P()),
        out_specs=(P("gy", "gx"), P("gy", "gx"), P("gy", None)),
        check_vma=False,
    )
```
